256 devices in a mesh: bl: 32 (over z, x), ch: 8 (over y, core).
Axes of the slice: x: 4, y: 4, z: 8, core: 2. Of those that a mesh axis runs over, the one named last changes fastest.
Arguments:
- visibility: float32 [2, 2048, 64, 128], P(None, 'bl', 'ch'), may hold values from -3 to 3
- coordinates: float32 [2, 2048, 128], P(None, 'bl'), may hold values from -10 to 10
- freq_ratio: float32 [64], P('ch'), may hold values from 0.75 to 1.25
- aterms: float32 [512, 2048], P('bl'), may hold values from -4 to 4
- stations: int32 [2048, 2], P('bl'), may hold values from 0 to 511
- sub_tile: int32 [2048], P('bl'), may hold values from 0 to 31, as said below
- offsets: int32 [2048, 2], P('bl'), may hold values from 0 to 224
- tile_of_slot: int32 [32], replicated, may hold values from 0 to 31, each once
Outputs:
- grid_tiles: float32 [32, 256, 4, 256], P('bl', 'ch')
The draws below stay inside these ranges and needn't reach their ends.
Inputs may be any that keep to these rules, and one draw needn't show every extreme that they name: `sub_tile`: within the rows of one device of bl no tile number appears more than 8 times, and one tile number, common to all devices, appears exactly 8 times in the rows of every device. `tile_of_slot`: each tile number appears once.
All inputs are finite; a program needn't handle non-finite values.
Results may differ from the reference program's by a relative error of at most 0.000098.
Values sent between devices are 32-bit elements; how exact they have to be, the bound alone decides.
No kernel may reach another device: no remote copies, remote signals or barrier semaphores. Data moves between devices by JAX's collectives and lax.ppermute only.
A program may use at most 128 MiB of HBM per device.

```python
import math
import jax
import jax.numpy as jnp
from jax import lax

STATIONS = 512
SUB = 32
TIMES = 128
SUB_DEV = 64
TILE = 256
SUBGRIDS = 2048
CHANNELS = 64
NTILES = 32
CAP = 8


def draw_sub_tile(key, part):
    blocks = SUBGRIDS // SUB_DEV
    common = jax.random.randint(jax.random.fold_in(key, 11), (), 0, NTILES).astype(jnp.int32)

    def one_block(block_key):
        order = jax.random.permutation(block_key, (NTILES - 1) * CAP)
        others = (order[:SUB_DEV - CAP] // CAP).astype(jnp.int32)
        others = others + (others >= common).astype(jnp.int32)
        chosen = jnp.concatenate([jnp.full((CAP,), common, jnp.int32), others])
        shuffle = jax.random.permutation(jax.random.fold_in(block_key, 7), SUB_DEV)
        return chosen[shuffle]
    block_keys = jax.random.split(jax.random.fold_in(key, 23), blocks)
    return jax.vmap(one_block)(block_keys).reshape(SUBGRIDS).astype(jnp.int32)


def plant(drawn, stream_key, smallest, largest):
    shape = drawn.shape
    index_at = [jax.random.randint(jax.random.fold_in(stream_key, axis), (), 0, shape[axis]) for axis in range(len(shape))]
    drawn = drawn.at[tuple(index_at)].set(smallest)
    longest = shape.index(max(shape))
    index_at[longest] = (index_at[longest] + 1) % shape[longest]
    return drawn.at[tuple(index_at)].set(largest)


def block_levels(stream_key, dims, cuts, smallest, high):
    level, own = 1.0, jax.random.fold_in(stream_key, 6)
    for position, shards_of in cuts:
        steps = jnp.exp(jax.random.uniform(jax.random.fold_in(own, position), (shards_of,), jnp.float32, smallest / len(cuts), high / len(cuts)))
        level = level * jnp.repeat(steps, dims[position] // shards_of).reshape([-1 if axis == position else 1 for axis in range(len(dims))])
    return level


def normal_values(key, dims, deviation, most, shards=(), kind=jnp.bfloat16):
    level = block_levels(key, dims, shards, -0.22, 0.18) if shards else 1.0
    values = jax.random.normal(key, dims, jnp.float32) * deviation * level
    return jnp.minimum(jnp.maximum(values, -most), most).astype(kind)


def setup_inputs(seed: int = 0) -> dict:
    seeds = jax.random.split(jax.random.key(seed), 9)
    return {
        "visibility": normal_values(seeds[0], (2, SUBGRIDS, CHANNELS, TIMES), 0.5, 3.0, ((1, 32), (2, 8)), jnp.float32),
        "coordinates": jnp.clip(jax.random.uniform(seeds[1], (2, SUBGRIDS, TIMES), jnp.float32, -10.0, 10.0) * block_levels(seeds[1], (2, SUBGRIDS, TIMES), ((1, 32),), -0.4, 0.0), -10.0, 10.0),
        "freq_ratio": jnp.clip(0.75 + 0.5 * jax.random.uniform(seeds[2], (CHANNELS,), jnp.float32) ** block_levels(seeds[2], (CHANNELS,), ((0, 8),), -0.2, 0.2), 0.75, 1.25),
        "aterms": normal_values(seeds[3], (STATIONS, 2 * SUB * SUB), 1.0, 4.0, ((0, 32),), jnp.float32),
        "stations": plant(jax.random.randint(seeds[4], (SUBGRIDS, 2), 0, STATIONS), jax.random.fold_in(seeds[4], 1), 0, STATIONS - 1).astype(jnp.int32),
        "sub_tile": draw_sub_tile(jax.random.fold_in(seeds[8], 71), 0),
        "offsets": plant(jax.random.randint(seeds[6], (SUBGRIDS, 2), 0, TILE - SUB + 1), jax.random.fold_in(seeds[6], 1), 0, TILE - SUB).astype(jnp.int32),
        "tile_of_slot": jax.random.permutation(seeds[7], NTILES).astype(jnp.int32),
    }


precise = lax.Precision.HIGHEST
full_turn = 2.0 * math.pi


def subgrid_images(visibility, coordinates, freq_ratio):
    block_size = visibility.shape[1]
    channels = visibility.shape[2]
    samples = visibility.shape[3]
    flat = channels * samples
    positions = (jnp.arange(SUB, dtype=jnp.float32) - SUB / 2) / SUB
    u_cells = (coordinates[0][:, None, :] * freq_ratio[None, :, None]).reshape(block_size, flat)
    v_cells = (coordinates[1][:, None, :] * freq_ratio[None, :, None]).reshape(block_size, flat)
    u_phase = full_turn * u_cells[:, :, None] * positions[None, None, :]
    v_phase = full_turn * v_cells[:, :, None] * positions[None, None, :]
    cos_u = jnp.cos(u_phase)
    sin_u = jnp.sin(u_phase)
    taylor = jnp.stack([jnp.ones_like(freq_ratio), 4.0 * (freq_ratio - 1.0)])
    weights = jnp.broadcast_to(taylor[:, :, None], (2, channels, samples)).reshape(2, flat)
    vis_real = visibility[0].reshape(block_size, flat)[:, :, None]
    vis_imag = visibility[1].reshape(block_size, flat)[:, :, None]
    left_real = vis_real * cos_u - vis_imag * sin_u
    left_imag = vis_real * sin_u + vis_imag * cos_u
    left_terms = jnp.stack([left_real, left_imag], 2)
    left_terms = (jnp.transpose(weights)[None, :, :, None, None] * left_terms[:, :, None, :, :]).reshape(block_size, flat, 4 * SUB)
    right_terms = jnp.stack([jnp.cos(v_phase), jnp.sin(v_phase)], 2).reshape(block_size, flat, 2 * SUB)
    product = jnp.einsum("ska,skb->sab", left_terms, right_terms, precision=precise).reshape(block_size, 2, 2, SUB, 2, SUB)
    real_part = product[:, :, 0, :, 0, :] - product[:, :, 1, :, 1, :]
    imag_part = product[:, :, 0, :, 1, :] + product[:, :, 1, :, 0, :]
    return real_part, imag_part


def finish(real_part, imag_part, a_first, a_second):
    block_size = real_part.shape[0]
    pixels = SUB * SUB
    first_real = a_first[:, :pixels].reshape(block_size, SUB, SUB)
    first_imag = a_first[:, pixels:].reshape(block_size, SUB, SUB)
    second_real = a_second[:, :pixels].reshape(block_size, SUB, SUB)
    second_imag = a_second[:, pixels:].reshape(block_size, SUB, SUB)
    pair_real = first_real * second_real + first_imag * second_imag
    pair_imag = first_imag * second_real - first_real * second_imag
    indices = jnp.arange(SUB, dtype=jnp.float32)
    taper_line = jnp.sin(math.pi * (indices + 0.5) / SUB)
    taper = taper_line[:, None] * taper_line[None, :]
    pair_real = (pair_real * taper)[:, None]
    pair_imag = (pair_imag * taper)[:, None]
    weighted_real = real_part * pair_real - imag_part * pair_imag
    weighted_imag = real_part * pair_imag + imag_part * pair_real
    centred = indices - SUB / 2
    angles = -full_turn * centred[:, None] * centred[None, :] / SUB
    four_real = jnp.cos(angles) / SUB
    four_imag = jnp.sin(angles) / SUB
    half_real = jnp.einsum("ja,stab->stjb", four_real, weighted_real, precision=precise) - jnp.einsum("ja,stab->stjb", four_imag, weighted_imag, precision=precise)
    half_imag = jnp.einsum("ja,stab->stjb", four_real, weighted_imag, precision=precise) + jnp.einsum("ja,stab->stjb", four_imag, weighted_real, precision=precise)
    full_real = jnp.einsum("stjb,kb->stjk", half_real, four_real, precision=precise) - jnp.einsum("stjb,kb->stjk", half_imag, four_imag, precision=precise)
    full_imag = jnp.einsum("stjb,kb->stjk", half_real, four_imag, precision=precise) + jnp.einsum("stjb,kb->stjk", half_imag, four_real, precision=precise)
    return jnp.stack([full_real, full_imag], 2).reshape(block_size, 4, SUB, SUB)


def reference(visibility, coordinates, freq_ratio, aterms, stations, sub_tile, offsets, tile_of_slot):
    blocks = SUBGRIDS // 16
    vis_blocks = visibility.reshape(2, blocks, 16, CHANNELS, TIMES).transpose(1, 0, 2, 3, 4)
    coord_blocks = coordinates.reshape(2, blocks, 16, TIMES).transpose(1, 0, 2, 3)
    station_blocks = stations.reshape(blocks, 16, 2)

    def one_block(pieces):
        vis_piece, coord_piece, station_piece = pieces
        real_part, imag_part = subgrid_images(vis_piece, coord_piece, freq_ratio)
        return finish(real_part, imag_part, aterms[station_piece[:, 0]], aterms[station_piece[:, 1]])

    subgrids = lax.map(one_block, (vis_blocks, coord_blocks, station_blocks)).reshape(SUBGRIDS, 4, SUB, SUB)
    tiles = jnp.zeros((NTILES, 4, TILE, TILE), jnp.float32)

    def place(index, tiles):
        corner = (sub_tile[index].astype(jnp.int32), jnp.int32(0), offsets[index, 0].astype(jnp.int32), offsets[index, 1].astype(jnp.int32))
        before = lax.dynamic_slice(tiles, corner, (1, 4, SUB, SUB))
        return lax.dynamic_update_slice(tiles, before + subgrids[index][None], corner)

    tiles = lax.fori_loop(0, SUBGRIDS, place, tiles)
    return jnp.transpose(tiles[tile_of_slot], (0, 2, 1, 3))
```

```python
import functools
import math

import jax
import jax.numpy as jnp
import numpy as np
from jax import lax
from jax.experimental import pallas as pl
from jax.experimental.pallas import tpu as pltpu
from jax.sharding import PartitionSpec as P

SUB = 32
TILE = 256
F32 = jnp.float32
BF16 = jnp.bfloat16
VM = pl.BlockSpec(memory_space=pltpu.VMEM)
SM = pl.BlockSpec(memory_space=pltpu.SMEM)

INV, TILES, ST0, ST1, OFF0, OFF1, OWN, ME = 0, 64, 128, 192, 256, 320, 384, 416

SIN = [(-1.0) ** k / math.factorial(2 * k + 1) for k in range(7)]
COS = [(-1.0) ** k / math.factorial(2 * k) for k in range(7)]


def poly(coefs, x2):
    r = jnp.full_like(x2, coefs[-1])
    for k in coefs[-2::-1]:
        r = r * x2 + k
    return r


def split(x):
    hi = x.astype(BF16)
    return hi, (x - hi.astype(F32)).astype(BF16)


def np_split(x):
    x = np.asarray(x, np.float64)
    hi = x.astype(np.float32).astype(BF16)
    lo = (x - hi.astype(np.float64)).astype(np.float32).astype(BF16)
    return hi, lo


def constants():
    pix = np.concatenate([16 + np.arange(16), 15 - np.arange(16)])
    m1 = np.zeros((2, 2, 2, 16, 2, 2, 32))
    m2 = np.zeros_like(m1)
    for b in range(32):
        n, sign = (b - 16, 1.0) if b >= 16 else (15 - b, -1.0)
        for k in range(2):
            for part in range(2):
                m1[k, part, 0, n, 0, k, b] = 1.0
                m1[k, part, 1, n, 1, k, b] = sign
                m2[k, part, 1, n, 0, k, b] = -sign
                m2[k, part, 0, n, 1, k, b] = 1.0
    to_image = np.concatenate([m1.reshape(128, 128), m2.reshape(128, 128)], 0)
    fold = np.zeros((2, 128, 128))
    for lane in range(128):
        for g in range(4):
            fold[0, lane, g * 32 + lane % 32] = 1.0
            fold[1, lane, g * 32 + lane % 32] = -1.0 if g < 2 else 1.0
    centred = np.arange(32) - 16
    four = np.exp(-2j * np.pi * centred[:, None] * centred[None, :] / 32) / 32
    left = np.concatenate([four.real[:, pix], four.imag[:, pix]], 1)
    lh, ll = np_split(left)
    left3 = np.concatenate([lh, ll, lh], 1)
    d = np.zeros((2, 2, 32, 2, 2, 32))
    for k in range(2):
        d[0, k, :, k, 0, :] = four.real.T
        d[1, k, :, k, 0, :] = -four.imag.T
        d[0, k, :, k, 1, :] = four.imag.T
        d[1, k, :, k, 1, :] = four.real.T
    dh, dl = np_split(d.reshape(128, 128))
    right3 = np.concatenate([dh, dl, dh], 0)
    line = np.sin(np.pi * (np.arange(32) + 0.5) / 32)
    taper = (line[:, None] * line[None, :]).reshape(8, 128).astype(np.float32)
    return (
        to_image.astype(BF16),
        fold.astype(BF16),
        left3.astype(BF16),
        right3.astype(BF16),
        taper,
    )


def pack_kernel(ints, freq, vis, coord, aterms, *outs):
    chunks, uv, shared = outs[:8], outs[8], outs[9]
    own = outs[10]
    me = ints[ME]
    y = me // 2
    core = me % 2
    row = lax.broadcasted_iota(jnp.int32, (8, 128), 0)
    lane = lax.broadcasted_iota(jnp.int32, (8, 128), 1)
    freqs = jnp.zeros((8, 128), F32)
    for k in range(8):
        freqs = jnp.where(row == k, freq[k], freqs)
    for q in range(8):
        to = ((y + q // 2) % 4) * 2 + (core + q % 2) % 2
        for j in range(8):
            s = ints[INV + 8 * j + to]
            chunks[q][j] = vis[0, s]
            chunks[q][8 + j] = vis[1, s]
        chunks[q][16] = freqs
    for n in range(32):
        own[ints[OWN + n]] = n
    blank = jnp.zeros((8, 128), F32)
    re = aterms[:, pl.ds(pl.multiple_of(me * 128, 128), 128)]
    im = aterms[:, pl.ds(pl.multiple_of(1024 + me * 128, 128), 128)]
    for b in range(32):
        shared[b, 0:16, :] = re
        shared[b, 16:32, :] = im
        shared[b, 32:40, :] = blank
    for j in range(8):
        s = ints[INV + 8 * j + me]
        for d in range(2):
            uv[d, pl.ds(j, 1), :] = coord[d, pl.ds(s, 1), :]
        spot = jnp.where(lane == 0, ints[OFF0 + s], jnp.where(lane == 1, ints[OFF1 + s], 0))
        shared[own[ints[TILES + s]], 32:40, :] = spot.astype(F32)


def image_kernel(count, first, uv, *refs):
    vis = refs[:count]
    refs = refs[count:]
    if not first:
        before = refs[0]
        refs = refs[1:]
    out, xu, xv, vp, lk, rk = refs
    for n in range(count):
        vref = vis[n]
        f = vref[16]
        weight = 4.0 * (f - 1.0)
        step = f * (math.pi / SUB)
        for s in range(8):
            base = []
            for d, table in ((0, xu), (1, xv)):
                phi = uv[d, pl.ds(s, 1), :] * step
                x2 = phi * phi
                zr = poly(COS, x2)
                zi = phi * poly(SIN, x2)
                wr = zr * zr - zi * zi
                wi = 2.0 * zr * zi
                cr, ci = zr, zi
                for m in range(16):
                    table[s, pl.ds(m * 8, 8), :] = cr
                    table[s, pl.ds((16 + m) * 8, 8), :] = ci
                    if m < 15:
                        cr, ci = cr * wr - ci * wi, cr * wi + ci * wr
                base.append((zr, zi))
            (ar, ai), (br, bi) = base
            pr = ar * br - ai * bi
            pi = ar * bi + ai * br
            vr = vref[s]
            vi = vref[8 + s]
            vp[s, 0] = vr * pr + vi * pi
            vp[s, 1] = vi * pr - vr * pi
        for s in range(8):
            for c in range(8):
                xs = xu[s, pl.ds(c, 32, stride=8), :]
                ys = xv[s, pl.ds(c, 32, stride=8), :]
                vr = vp[s, 0, pl.ds(c, 1), :]
                vi = vp[s, 1, pl.ds(c, 1), :]
                lh, ll = split(jnp.concatenate([xs * vr, xs * vi], 0))
                lk[s % 2, :, pl.ds(c * 256, 128)] = lh
                lk[s % 2, :, pl.ds(c * 256 + 128, 128)] = ll
                yh, yl = split(ys)
                wh, wl = split(ys * weight[c : c + 1])
                r4 = jnp.concatenate([yh, yl, wh, wl], 0)
                rk[s % 2, :, pl.ds(c * 256, 128)] = r4
                rk[s % 2, :, pl.ds(c * 256 + 128, 128)] = r4
            o = lax.dot_general(
                lk[s % 2], rk[s % 2], (((1,), (1,)), ((), ())), preferred_element_type=F32
            )
            if n == 0:
                out[s] = o if first else before[s] + o
            else:
                out[s] += o


def images(uv, chunks, before=None):
    count = len(chunks)
    first = before is None
    args = [uv, *chunks] + ([] if first else [before])
    return pl.pallas_call(
        functools.partial(image_kernel, count, first),
        out_shape=jax.ShapeDtypeStruct((8, 64, 128), F32),
        in_specs=[VM] * len(args),
        out_specs=VM,
        scratch_shapes=[
            pltpu.VMEM((8, 256, 128), F32),
            pltpu.VMEM((8, 256, 128), F32),
            pltpu.VMEM((8, 2, 8, 128), F32),
            pltpu.VMEM((2, 64, 2048), BF16),
            pltpu.VMEM((2, 128, 2048), BF16),
        ],
        cost_estimate=pl.CostEstimate(
            flops=count * 60_000_000, bytes_accessed=count * 100_000, transcendentals=0
        ),
        name=f"image{count}",
    )(*args)


def pair_kernel(ints, table, taper, out):
    me = ints[ME]
    g = taper[pl.ds(me, 1), :]
    for to in range(8):
        for j in range(8):
            s = ints[INV + 8 * j + to]
            p = ints[ST0 + s]
            q = ints[ST1 + s]
            pr = table[p // 16, pl.ds(p % 16, 1), :]
            pi = table[p // 16, pl.ds(16 + p % 16, 1), :]
            qr = table[q // 16, pl.ds(q % 16, 1), :]
            qi = table[q // 16, pl.ds(16 + q % 16, 1), :]
            out[to, pl.ds(j, 1), :] = (pr * qr + pi * qi) * g
            out[to, pl.ds(8 + j, 1), :] = (pi * qr - pr * qi) * g


def finish_kernel(ints, acc, pair, to_image, fold, left3, right3, out, own):
    me = ints[ME]
    for n in range(32):
        own[ints[OWN + n]] = n
    blank = jnp.zeros((32, 128), F32)
    for b in range(32):
        out[b] = blank
    row = lax.broadcasted_iota(jnp.int32, (8, 128), 0)
    group = lax.broadcasted_iota(jnp.int32, (8, 128), 1) // 32
    low = group == row % 4
    high = group == 3 - row % 4
    spread = [[], []]
    halves = []
    for s in range(8):
        for r in range(2):
            rows = [jnp.broadcast_to(pair[c, pl.ds(8 * r + s, 1), :], (8, 128)) for c in range(8)]
            for c in (4, 6):
                spread[r].append(jnp.where(low, jnp.where(row < 4, rows[c], rows[c + 1]), 0.0))
            for c in (3, 1):
                spread[r].append(jnp.where(high, jnp.where(row < 4, rows[c], rows[c - 1]), 0.0))
        g = acc[s]
        rc, rs, ic, js = g[0:16], g[16:32], g[32:48], g[48:64]
        real = jnp.concatenate([rc - js, rc + js], 0)
        imag = jnp.concatenate([ic + rs, ic - rs], 0)
        halves.append(jnp.concatenate([real, imag], 1))
    stack = jnp.concatenate(halves, 0)
    sh, sl = split(stack)
    img = jnp.dot(sh, to_image[...], preferred_element_type=F32) + jnp.dot(
        sl, to_image[...], preferred_element_type=F32
    )

    def unfold(r):
        h, l = split(jnp.concatenate(spread[r], 0))
        return jnp.dot(h, fold[r], preferred_element_type=F32) + jnp.dot(
            l, fold[r], preferred_element_type=F32
        )

    weighted = img * unfold(0) + pltpu.roll(img, 64, 1) * unfold(1)
    sign = jnp.where(lax.broadcasted_iota(jnp.int32, (256, 128), 1) < 64, -1.0, 1.0)
    turned = pltpu.roll(weighted, 64, 1) * sign
    wh, wl = split(weighted)
    th, tl = split(turned)

    def lanes(x):
        return jnp.concatenate([x[32 * s : 32 * s + 32] for s in range(8)], 1)

    wh, wl, th, tl = lanes(wh), lanes(wl), lanes(th), lanes(tl)
    rhs = jnp.concatenate([wh, th, wh, th, wl, tl], 0)
    half = jnp.dot(left3[...], rhs, preferred_element_type=F32)
    half = jnp.concatenate([half[:, 128 * s : 128 * s + 128] for s in range(8)], 0)
    hh, hl = split(half)
    full = jnp.dot(
        jnp.concatenate([hh, hh, hl], 1), right3[...], preferred_element_type=F32
    )
    for s in range(8):
        out[own[ints[TILES + ints[INV + 8 * s + me]]]] = full[32 * s : 32 * s + 32]


def place_kernel(spots, me_ref, arrived, keep, give, acc):
    lane = lax.broadcasted_iota(jnp.int32, (32, 128), 1)
    me = me_ref[0]
    y = me // 2
    core = me % 2
    acc[...] = jnp.zeros_like(acc)

    def one(i, unused):
        r = spots[2 * i]
        c = spots[2 * i + 1]
        tile = arrived[i]
        near = (lane >= c) & (lane < c + 32)
        far = (lane + 128 >= c) & (lane + 128 < c + 32)
        for m in range(4):
            moved = pltpu.roll(tile, (c - 32 * m + 128) % 128, 1)
            for half, mask in ((0, near), (1, far)):
                at = (2 * m + half, pl.ds(r, 32), slice(None))
                acc[at] = acc[at] + jnp.where(mask, moved, 0.0)
        return unused

    lax.fori_loop(0, 32, one, 0)
    for d in range(4):
        block = ((y + d) % 4) * 2
        for k in range(8):
            keep[d, k] = acc[k, pl.ds(pl.multiple_of((block + core) * 32, 32), 32), :]
            give[d, k] = acc[k, pl.ds(pl.multiple_of((block + 1 - core) * 32, 32), 32), :]


def merge_kernel(keep, got, *outs):
    for d in range(4):
        outs[d][...] = keep[d] + got[d]


def last_kernel(a, b, c, d, out):
    for m in range(4):
        for half in range(2):
            k = 2 * m + half
            out[0, :, m, 128 * half : 128 * half + 128] = (a[k] + b[k]) + (c[k] + d[k])


def shift(x, dy, dc):
    pairs = [(i, ((i // 2 + dy) % 4) * 2 + (i + dc) % 2) for i in range(8)]
    return lax.ppermute(x, "ch", pairs)


def local(visibility, coordinates, freq_ratio, aterms, stations, sub_tile, offsets, tile_of_slot):
    to_image, fold, left3, right3, taper = constants()
    me = lax.axis_index("ch").astype(jnp.int32)
    order = jnp.arange(64, dtype=jnp.int32)
    key = sub_tile * 64 + order
    pos = jnp.sum((key[None, :] < key[:, None]).astype(jnp.int32), axis=1)
    inv = jnp.sum(jnp.where(pos[None, :] == order[:, None], order[None, :], 0), axis=1)
    ints = jnp.concatenate(
        [
            inv,
            sub_tile,
            stations[:, 0],
            stations[:, 1],
            offsets[:, 0],
            offsets[:, 1],
            tile_of_slot,
            me[None],
        ]
    )
    packed = pl.pallas_call(
        pack_kernel,
        out_shape=[jax.ShapeDtypeStruct((17, 8, 128), F32)] * 8
        + [jax.ShapeDtypeStruct((2, 8, 128), F32), jax.ShapeDtypeStruct((32, 40, 128), F32)],
        in_specs=[SM, SM, VM, VM, VM],
        out_specs=[VM] * 10,
        scratch_shapes=[pltpu.SMEM((32,), jnp.int32)],
        name="pack",
    )(ints, freq_ratio, visibility, coordinates, aterms)
    chunks, uv, shared = packed[:8], packed[8], packed[9]
    moved = [shift(chunks[q], q // 2, q % 2) for q in range(1, 8)]
    table = lax.all_to_all(shared.reshape(32, 40 * 128), "bl", 0, 0, tiled=True)
    table = table.reshape(32, 40, 128)
    acc = images(uv, [chunks[0]])
    acc = images(uv, [moved[0]], acc)
    acc = images(uv, [moved[1], moved[2], moved[5], moved[6]], acc)
    pair = pl.pallas_call(
        pair_kernel,
        out_shape=jax.ShapeDtypeStruct((8, 16, 128), F32),
        in_specs=[SM, VM, VM],
        out_specs=VM,
        name="pair",
    )(ints, table, taper)
    pair = lax.all_to_all(pair.reshape(8, 2048), "ch", 0, 0, tiled=True).reshape(8, 16, 128)
    acc = images(uv, [moved[3], moved[4]], acc)
    outgoing = pl.pallas_call(
        finish_kernel,
        out_shape=jax.ShapeDtypeStruct((32, 32, 128), F32),
        in_specs=[SM] + [VM] * 6,
        out_specs=VM,
        scratch_shapes=[pltpu.SMEM((32,), jnp.int32)],
        name="finish",
    )(ints, acc, pair, to_image, fold, left3, right3)
    arrived = lax.all_to_all(outgoing.reshape(32, 4096), "bl", 0, 0, tiled=True)
    arrived = arrived.reshape(32, 32, 128)
    spots = table[:, 32, 0:2].reshape(64).astype(jnp.int32)
    half = jax.ShapeDtypeStruct((4, 8, 32, 128), F32)
    keep, give = pl.pallas_call(
        place_kernel,
        out_shape=[half, half],
        in_specs=[SM, SM, VM],
        out_specs=[VM, VM],
        scratch_shapes=[pltpu.VMEM((8, TILE, 128), F32)],
        name="place",
    )(spots, me[None], arrived)
    got = shift(give, 0, 1)
    block = jax.ShapeDtypeStruct((8, 32, 128), F32)
    sums = pl.pallas_call(
        merge_kernel,
        out_shape=[block] * 4,
        in_specs=[VM, VM],
        out_specs=[VM] * 4,
        name="merge",
    )(keep, got)
    parts = [sums[0]] + [shift(sums[d], d, 0) for d in range(1, 4)]
    return pl.pallas_call(
        last_kernel,
        out_shape=jax.ShapeDtypeStruct((1, 32, 4, TILE), F32),
        in_specs=[VM] * 4,
        out_specs=VM,
        name="last",
    )(*parts)


def solution(mesh):
    placed = (
        P(None, "bl", "ch", None),
        P(None, "bl", None),
        P("ch"),
        P("bl", None),
        P("bl", None),
        P("bl"),
        P("bl", None),
        P(),
    )
    return jax.shard_map(
        local, mesh=mesh, in_specs=placed, out_specs=P("bl", "ch", None, None), check_vma=False
    )
```

```python
import functools
import math

import jax
import jax.numpy as jnp
import numpy as np
from jax import lax
from jax.experimental import pallas as pl
from jax.experimental.pallas import tpu as pltpu
from jax.sharding import PartitionSpec as P

SUB = 32
TILE = 256
F32 = jnp.float32
BF16 = jnp.bfloat16
VM = pl.BlockSpec(memory_space=pltpu.VMEM)
SM = pl.BlockSpec(memory_space=pltpu.SMEM)

SIN = [(-1.0) ** k / math.factorial(2 * k + 1) for k in range(7)]
COS = [(-1.0) ** k / math.factorial(2 * k) for k in range(7)]


def poly(coefs, x2):
    r = jnp.full_like(x2, coefs[-1])
    for k in coefs[-2::-1]:
        r = r * x2 + k
    return r


def split(x):
    hi = x.astype(BF16)
    return hi, (x - hi.astype(F32)).astype(BF16)


def np_split(x):
    x = np.asarray(x, np.float64)
    hi = x.astype(np.float32).astype(BF16)
    lo = (x - hi.astype(np.float64)).astype(np.float32).astype(BF16)
    return hi, lo


def constants():
    pix = np.concatenate([16 + np.arange(16), 15 - np.arange(16)])
    m1 = np.zeros((2, 2, 2, 16, 2, 2, 32))
    m2 = np.zeros_like(m1)
    for b in range(32):
        n, sign = (b - 16, 1.0) if b >= 16 else (15 - b, -1.0)
        for k in range(2):
            for part in range(2):
                m1[part, k, 0, n, 0, k, b] = 1.0
                m1[part, k, 1, n, 1, k, b] = sign
                m2[part, k, 1, n, 0, k, b] = -sign
                m2[part, k, 0, n, 1, k, b] = 1.0
    to_image = np.concatenate([m1.reshape(128, 128), m2.reshape(128, 128)], 0)
    fold = np.zeros((2, 128, 128))
    for lane in range(128):
        for g in range(4):
            fold[0, lane, g * 32 + lane % 32] = 1.0
            fold[1, lane, g * 32 + lane % 32] = -1.0 if g < 2 else 1.0
    centred = np.arange(32) - 16
    four = np.exp(-2j * np.pi * centred[:, None] * centred[None, :] / 32) / 32
    left = np.concatenate([four.real[:, pix], four.imag[:, pix]], 1)
    lh, ll = np_split(left)
    left3 = np.concatenate([lh, ll, lh], 1)
    d = np.zeros((2, 2, 32, 2, 2, 32))
    for k in range(2):
        d[0, k, :, k, 0, :] = four.real.T
        d[1, k, :, k, 0, :] = -four.imag.T
        d[0, k, :, k, 1, :] = four.imag.T
        d[1, k, :, k, 1, :] = four.real.T
    dh, dl = np_split(d.reshape(128, 128))
    right3 = np.concatenate([dh, dl, dh], 0)
    line = np.sin(np.pi * (np.arange(32) + 0.5) / 32)
    taper = (line[:, None] * line[None, :]).reshape(8, 128).astype(np.float32)
    return (
        to_image.astype(BF16),
        fold.astype(BF16),
        left3.astype(BF16),
        right3.astype(BF16),
        taper,
    )


def owners(slots, own):
    for n in range(32):
        own[slots[n]] = n


def share_kernel(me_ref, inv, tiles, offs, slots, aterms, shared, own):
    me = me_ref[0]
    owners(slots, own)
    lane = lax.broadcasted_iota(jnp.int32, (1, 128), 1)
    re = aterms[:, pl.ds(pl.multiple_of(me * 128, 128), 128)]
    im = aterms[:, pl.ds(pl.multiple_of(1024 + me * 128, 128), 128)]
    blank = jnp.zeros((1, 128), F32)
    for b in range(32):
        shared[33 * b : 33 * b + 16, :] = re
        shared[33 * b + 16 : 33 * b + 32, :] = im
        shared[33 * b + 32 : 33 * b + 33, :] = blank
    for j in range(8):
        s = inv[8 * j + me]
        spot = jnp.where(lane == 0, offs[0, s], jnp.where(lane == 1, offs[1, s], 0))
        shared[pl.ds(33 * own[tiles[s]] + 32, 1), :] = spot.astype(F32)


def pack_kernel(me_ref, inv, freq, vis, coord, *outs):
    uv = outs[5]
    me = me_ref[0]
    y = me >> 1
    core = me & 1
    row = lax.broadcasted_iota(jnp.int32, (8, 128), 0)
    freqs = jnp.zeros((8, 128), F32)
    for k in range(8):
        freqs = jnp.where(row == k, freq[k], freqs)
    places = [outs[0], outs[1]] + [outs[1 + d].at[e] for d in range(1, 4) for e in range(2)]
    for q in range(8):
        to = (((y + q // 2) & 3) << 1) + ((core + q % 2) & 1)
        for j in range(8):
            s = inv[8 * j + to]
            places[q][j] = vis[0, s]
            places[q][8 + j] = vis[1, s]
        places[q][16] = freqs
    for j in range(8):
        s = inv[8 * j + me]
        for d in range(2):
            uv[d, pl.ds(j, 1), :] = coord[d, pl.ds(s, 1), :]


def image_kernel(picks, first, uv, *refs):
    count = len(picks)
    vis = [r if p is None else r.at[p] for p, r in zip(picks, refs)]
    refs = refs[count:]
    if not first:
        before = refs[0]
        refs = refs[1:]
    out, xu, xv, vp = refs
    for n in range(count):
        vref = vis[n]
        f = vref[16]
        weight = 4.0 * (f - 1.0)
        step = f * (math.pi / SUB)
        for s in range(8):
            base = []
            for d, table in ((0, xu), (1, xv)):
                phi = uv[d, pl.ds(s, 1), :] * step
                x2 = phi * phi
                zr = poly(COS, x2)
                zi = phi * poly(SIN, x2)
                wr = zr * zr - zi * zi
                wi = 2.0 * zr * zi
                cr, ci = zr, zi
                for m in range(16):
                    table[s, pl.ds(m * 8, 8), :] = cr
                    table[s, pl.ds((16 + m) * 8, 8), :] = ci
                    if m < 15:
                        cr, ci = cr * wr - ci * wi, cr * wi + ci * wr
                base.append((zr, zi))
            (ar, ai), (br, bi) = base
            pr = ar * br - ai * bi
            pi = ar * bi + ai * br
            vr = vref[s]
            vi = vref[8 + s]
            vp[s, 0] = vr * pr + vi * pi
            vp[s, 1] = vi * pr - vr * pi
        for s in range(8):
            lefts, rights = [], []
            for c in range(8):
                xs = xu[s, pl.ds(c, 32, stride=8), :]
                ys = xv[s, pl.ds(c, 32, stride=8), :]
                vr = vp[s, 0, pl.ds(c, 1), :]
                vi = vp[s, 1, pl.ds(c, 1), :]
                lefts.append(jnp.concatenate(split(jnp.concatenate([xs * vr, xs * vi], 0)), 0))
                both = jnp.concatenate([ys, ys * weight[c : c + 1]], 0)
                rights.append(jnp.concatenate(split(both), 0))
            o = lax.dot_general(
                jnp.concatenate(lefts, 1),
                jnp.concatenate(rights, 1),
                (((1,), (1,)), ((), ())),
                preferred_element_type=F32,
            )
            o = o[:64] + o[64:]
            if n == 0:
                out[s] = o if first else before[s] + o
            else:
                out[s] += o


def grant(mib):
    return pltpu.CompilerParams(vmem_limit_bytes=mib << 20)


def images(uv, chunks, before=None):
    picks = tuple(p for _, p in chunks)
    count = len(chunks)
    first = before is None
    args = [uv] + [c for c, _ in chunks] + ([] if first else [before])
    return pl.pallas_call(
        functools.partial(image_kernel, picks, first),
        out_shape=jax.ShapeDtypeStruct((8, 64, 128), F32),
        in_specs=[VM] * len(args),
        out_specs=VM,
        scratch_shapes=[
            pltpu.VMEM((8, 256, 128), F32),
            pltpu.VMEM((8, 256, 128), F32),
            pltpu.VMEM((8, 2, 8, 128), F32),
        ],
        compiler_params=grant(16),
        cost_estimate=pl.CostEstimate(
            flops=count * 200_000_000, bytes_accessed=count * 100_000, transcendentals=0
        ),
        name=f"image{count}",
    )(*args)


def pair_kernel(me_ref, inv, stations, table, taper, out):
    g = taper[pl.ds(me_ref[0], 1), :]
    for to in range(8):
        for j in range(8):
            s = inv[8 * j + to]
            p = stations[0, s]
            q = stations[1, s]
            p = p + 17 * (p >> 4)
            q = q + 17 * (q >> 4)
            pr = table[pl.ds(p, 1), :]
            pi = table[pl.ds(p + 16, 1), :]
            qr = table[pl.ds(q, 1), :]
            qi = table[pl.ds(q + 16, 1), :]
            out[to, pl.ds(j, 1), :] = (pr * qr + pi * qi) * g
            out[to, pl.ds(8 + j, 1), :] = (pi * qr - pr * qi) * g


def finish_kernel(me_ref, inv, tiles, slots, acc, pair, to_image, fold, left3, right3, out, own):
    me = me_ref[0]
    owners(slots, own)
    blank = jnp.zeros((32, 128), F32)
    for b in range(32):
        out[b] = blank
    row = lax.broadcasted_iota(jnp.int32, (8, 128), 0)
    group = lax.broadcasted_iota(jnp.int32, (8, 128), 1) // 32
    low = group == row % 4
    high = group == 3 - row % 4
    spread = [[], []]
    halves = []
    for s in range(8):
        for r in range(2):
            rows = [jnp.broadcast_to(pair[c, pl.ds(8 * r + s, 1), :], (8, 128)) for c in range(8)]
            for c in (4, 6):
                spread[r].append(jnp.where(low, jnp.where(row < 4, rows[c], rows[c + 1]), 0.0))
            for c in (3, 1):
                spread[r].append(jnp.where(high, jnp.where(row < 4, rows[c], rows[c - 1]), 0.0))
        g = acc[s]
        rc, rs, ic, js = g[0:16], g[16:32], g[32:48], g[48:64]
        real = jnp.concatenate([rc - js, rc + js], 0)
        imag = jnp.concatenate([ic + rs, ic - rs], 0)
        halves.append(jnp.concatenate([real, imag], 1))
    stack = jnp.concatenate(halves, 0)
    sh, sl = split(stack)
    img = jnp.dot(sh, to_image[...], preferred_element_type=F32) + jnp.dot(
        sl, to_image[...], preferred_element_type=F32
    )

    def unfold(r):
        h, l = split(jnp.concatenate(spread[r], 0))
        return jnp.dot(h, fold[r], preferred_element_type=F32) + jnp.dot(
            l, fold[r], preferred_element_type=F32
        )

    weighted = img * unfold(0) + pltpu.roll(img, 64, 1) * unfold(1)
    sign = jnp.where(lax.broadcasted_iota(jnp.int32, (256, 128), 1) < 64, -1.0, 1.0)
    turned = pltpu.roll(weighted, 64, 1) * sign
    wh, wl = split(weighted)
    th, tl = split(turned)

    def lanes(x):
        return jnp.concatenate([x[32 * s : 32 * s + 32] for s in range(8)], 1)

    wh, wl, th, tl = lanes(wh), lanes(wl), lanes(th), lanes(tl)
    rhs = jnp.concatenate([wh, th, wh, th, wl, tl], 0)
    half = jnp.dot(left3[...], rhs, preferred_element_type=F32)
    half = jnp.concatenate([half[:, 128 * s : 128 * s + 128] for s in range(8)], 0)
    hh, hl = split(half)
    full = jnp.dot(
        jnp.concatenate([hh, hh, hl], 1), right3[...], preferred_element_type=F32
    )
    for s in range(8):
        out[own[tiles[inv[8 * s + me]]]] = full[32 * s : 32 * s + 32]


def place_kernel(me_ref, spots, arrived, keep, give, acc):
    lane = lax.broadcasted_iota(jnp.int32, (32, 128), 1)
    me = me_ref[0]
    y = me >> 1
    core = me & 1
    acc[...] = jnp.zeros_like(acc)

    def one(i, unused):
        r = spots[2 * i]
        c = spots[2 * i + 1]
        half = c >> 7
        c = c & 127
        tile = arrived[i]
        near = (lane >= c) & (lane < c + 32)
        moved = [pltpu.roll(tile, (c - 32 * m) & 127, 1) for m in range(4)]
        for m in range(4):
            at = (2 * m + half, pl.ds(r, 32), slice(None))
            acc[at] = acc[at] + jnp.where(near, moved[m], 0.0)

        @pl.when(c > 96)
        def _():
            far = lane < c - 96
            for m in range(4):
                at = (2 * m + 1, pl.ds(r, 32), slice(None))
                acc[at] = acc[at] + jnp.where(far, moved[m], 0.0)

        return unused

    lax.fori_loop(0, 32, one, 0)
    for d in range(4):
        block = ((y + d) & 3) << 1
        for k in range(8):
            keep[d, k] = acc[k, pl.ds(pl.multiple_of((block + core) * 32, 32), 32), :]
            give[d, k] = acc[k, pl.ds(pl.multiple_of((block + 1 - core) * 32, 32), 32), :]


def merge_kernel(keep, got, *outs):
    for d in range(4):
        outs[d][...] = keep[d] + got[d]


def last_kernel(a, b, c, d, out):
    for m in range(4):
        for half in range(2):
            k = 2 * m + half
            out[0, :, m, 128 * half : 128 * half + 128] = (a[k] + b[k]) + (c[k] + d[k])


def shift(x, dy, dc):
    pairs = [(i, ((i // 2 + dy) % 4) * 2 + (i + dc) % 2) for i in range(8)]
    return lax.ppermute(x, "ch", pairs)


def local(visibility, coordinates, freq_ratio, aterms, stations, sub_tile, offsets, tile_of_slot):
    to_image, fold, left3, right3, taper = constants()
    me = lax.axis_index("ch").astype(jnp.int32)
    me = me[None]
    order = jnp.arange(64, dtype=jnp.int32)
    key = sub_tile * 64 + order
    pos = jnp.sum((key[None, :] < key[:, None]).astype(jnp.int32), axis=1)
    inv = jnp.sum(jnp.where(pos[None, :] == order[:, None], order[None, :], 0), axis=1)
    stations = stations.T
    offsets = offsets.T
    own = pltpu.SMEM((32,), jnp.int32)
    shared = pl.pallas_call(
        share_kernel,
        out_shape=jax.ShapeDtypeStruct((33 * 32, 128), F32),
        in_specs=[SM] * 5 + [VM],
        out_specs=VM,
        scratch_shapes=[own],
        compiler_params=grant(4),
        name="share",
    )(me, inv, sub_tile, offsets, tile_of_slot, aterms)
    inv, shared = lax.optimization_barrier((inv, shared))
    table = lax.all_to_all(shared.reshape(32, 33 * 128), "bl", 0, 0, tiled=True)
    table = table.reshape(33 * 32, 128)
    chunk = jax.ShapeDtypeStruct((17, 8, 128), F32)
    double = jax.ShapeDtypeStruct((2, 17, 8, 128), F32)
    mine, near, *far, uv = pl.pallas_call(
        pack_kernel,
        out_shape=[chunk, chunk, double, double, double, jax.ShapeDtypeStruct((2, 8, 128), F32)],
        in_specs=[SM, SM, SM, VM, VM],
        out_specs=[VM] * 6,
        compiler_params=grant(8),
        name="pack",
    )(me, inv, freq_ratio, visibility, coordinates)
    near = shift(near, 0, 1)
    direct = [shift(far[d - 1], d, 0) for d in range(1, 4)]
    acc = images(uv, [(mine, None), (near, None)])
    acc, *direct = lax.optimization_barrier((acc, *direct))
    swapped = [shift(x, 0, 1) for x in direct]
    acc = images(uv, [(direct[0], 0), (direct[2], 0)], acc)
    acc = images(uv, [(swapped[0], 1), (swapped[2], 1), (direct[1], 0), (swapped[1], 1)], acc)
    acc, table = lax.optimization_barrier((acc, table))
    pair = pl.pallas_call(
        pair_kernel,
        out_shape=jax.ShapeDtypeStruct((8, 16, 128), F32),
        in_specs=[SM, SM, SM, VM, VM],
        out_specs=VM,
        compiler_params=grant(4),
        name="pair",
    )(me, inv, stations, table, taper)
    pair = lax.all_to_all(pair.reshape(8, 2048), "ch", 0, 0, tiled=True).reshape(8, 16, 128)
    outgoing = pl.pallas_call(
        finish_kernel,
        out_shape=jax.ShapeDtypeStruct((32, 32, 128), F32),
        in_specs=[SM] * 4 + [VM] * 6,
        out_specs=VM,
        scratch_shapes=[own],
        compiler_params=grant(12),
        name="finish",
    )(me, inv, sub_tile, tile_of_slot, acc, pair, to_image, fold, left3, right3)
    arrived = lax.all_to_all(outgoing.reshape(32, 4096), "bl", 0, 0, tiled=True)
    arrived = arrived.reshape(32, 32, 128)
    spots = table[32::33, 0:2].reshape(64).astype(jnp.int32)
    half = jax.ShapeDtypeStruct((4, 8, 32, 128), F32)
    keep, give = pl.pallas_call(
        place_kernel,
        out_shape=[half, half],
        in_specs=[SM, SM, VM],
        out_specs=[VM, VM],
        scratch_shapes=[pltpu.VMEM((8, TILE, 128), F32)],
        compiler_params=grant(8),
        name="place",
    )(me, spots, arrived)
    got = shift(give, 0, 1)
    block = jax.ShapeDtypeStruct((8, 32, 128), F32)
    sums = pl.pallas_call(
        merge_kernel,
        out_shape=[block] * 4,
        in_specs=[VM, VM],
        out_specs=[VM] * 4,
        compiler_params=grant(6),
        name="merge",
    )(keep, got)
    parts = [sums[0]] + [shift(sums[d], d, 0) for d in range(1, 4)]
    return pl.pallas_call(
        last_kernel,
        out_shape=jax.ShapeDtypeStruct((1, 32, 4, TILE), F32),
        in_specs=[VM] * 4,
        out_specs=VM,
        compiler_params=grant(4),
        name="last",
    )(*parts)


def solution(mesh):
    placed = (
        P(None, "bl", "ch", None),
        P(None, "bl", None),
        P("ch"),
        P("bl", None),
        P("bl", None),
        P("bl"),
        P("bl", None),
        P(),
    )
    return jax.shard_map(
        local, mesh=mesh, in_specs=placed, out_specs=P("bl", "ch", None, None), check_vma=False
    )
```

```python
import functools
import math

import jax
import jax.numpy as jnp
import numpy as np
from jax import lax
from jax.experimental import pallas as pl
from jax.experimental.pallas import tpu as pltpu
from jax.sharding import PartitionSpec as P

SUB = 32
TILE = 256
F32 = jnp.float32
BF16 = jnp.bfloat16
VM = pl.BlockSpec(memory_space=pltpu.VMEM)
SM = pl.BlockSpec(memory_space=pltpu.SMEM)

SIN = [(-1.0) ** k / math.factorial(2 * k + 1) for k in range(7)]
COS = [(-1.0) ** k / math.factorial(2 * k) for k in range(7)]


def poly(coefs, x2):
    r = jnp.full_like(x2, coefs[-1])
    for k in coefs[-2::-1]:
        r = r * x2 + k
    return r


def split(x):
    hi = x.astype(BF16)
    return hi, (x - hi.astype(F32)).astype(BF16)


def np_split(x):
    x = np.asarray(x, np.float64)
    hi = x.astype(np.float32).astype(BF16)
    lo = (x - hi.astype(np.float64)).astype(np.float32).astype(BF16)
    return hi, lo


def constants():
    pix = np.concatenate([16 + np.arange(16), 15 - np.arange(16)])
    m1 = np.zeros((2, 2, 2, 16, 2, 2, 32))
    m2 = np.zeros_like(m1)
    for b in range(32):
        n, sign = (b - 16, 1.0) if b >= 16 else (15 - b, -1.0)
        for k in range(2):
            for part in range(2):
                m1[part, k, 0, n, 0, k, b] = 1.0
                m1[part, k, 1, n, 1, k, b] = sign
                m2[part, k, 1, n, 0, k, b] = -sign
                m2[part, k, 0, n, 1, k, b] = 1.0
    to_image = np.concatenate([m1.reshape(128, 128), m2.reshape(128, 128)], 0)
    fold = np.zeros((2, 128, 128))
    for lane in range(128):
        for g in range(4):
            fold[0, lane, g * 32 + lane % 32] = 1.0
            fold[1, lane, g * 32 + lane % 32] = -1.0 if g < 2 else 1.0
    centred = np.arange(32) - 16
    four = np.exp(-2j * np.pi * centred[:, None] * centred[None, :] / 32) / 32
    left = np.concatenate([four.real[:, pix], four.imag[:, pix]], 1)
    lh, ll = np_split(left)
    left3 = np.concatenate([lh, ll, lh], 1)
    d = np.zeros((2, 2, 32, 2, 2, 32))
    for k in range(2):
        d[0, k, :, k, 0, :] = four.real.T
        d[1, k, :, k, 0, :] = -four.imag.T
        d[0, k, :, k, 1, :] = four.imag.T
        d[1, k, :, k, 1, :] = four.real.T
    dh, dl = np_split(d.reshape(128, 128))
    right3 = np.concatenate([dh, dl, dh], 0)
    line = np.sin(np.pi * (np.arange(32) + 0.5) / 32)
    taper = (line[:, None] * line[None, :]).reshape(8, 128).astype(np.float32)
    return (
        to_image.astype(BF16),
        fold.astype(BF16),
        left3.astype(BF16),
        right3.astype(BF16),
        taper,
    )


def owners(slots, own):
    for n in range(32):
        own[slots[n]] = n


def share_kernel(me_ref, aterms, shared):
    me = me_ref[0]
    re = aterms[:, pl.ds(pl.multiple_of(me * 128, 128), 128)]
    im = aterms[:, pl.ds(pl.multiple_of(1024 + me * 128, 128), 128)]
    for b in range(32):
        shared[b, 0:16, :] = re
        shared[b, 16:32, :] = im


def pack_kernel(me_ref, inv, freq, vis, coord, *outs):
    uv = outs[5]
    me = me_ref[0]
    y = me >> 1
    core = me & 1
    row = lax.broadcasted_iota(jnp.int32, (8, 128), 0)
    freqs = jnp.zeros((8, 128), F32)
    for k in range(8):
        freqs = jnp.where(row == k, freq[k], freqs)
    places = [outs[0], outs[1]] + [outs[1 + d].at[e] for d in range(1, 4) for e in range(2)]
    for q in range(8):
        to = (((y + q // 2) & 3) << 1) + ((core + q % 2) & 1)
        for j in range(8):
            s = inv[8 * j + to]
            places[q][j] = vis[0, s]
            places[q][8 + j] = vis[1, s]
        places[q][16] = freqs
    for j in range(8):
        s = inv[8 * j + me]
        for d in range(2):
            uv[d, pl.ds(j, 1), :] = coord[d, pl.ds(s, 1), :]


def image_kernel(picks, first, uv, *refs):
    count = len(picks)
    vis = [r if p is None else r.at[p] for p, r in zip(picks, refs)]
    refs = refs[count:]
    if not first:
        before = refs[0]
        refs = refs[1:]
    out, xu, xv, vp = refs
    for n in range(count):
        vref = vis[n]
        f = vref[16]
        weight = 4.0 * (f - 1.0)
        step = f * (math.pi / SUB)
        for s in range(8):
            base = []
            for d, table in ((0, xu), (1, xv)):
                phi = uv[d, pl.ds(s, 1), :] * step
                x2 = phi * phi
                zr = poly(COS, x2)
                zi = phi * poly(SIN, x2)
                wr = zr * zr - zi * zi
                wi = 2.0 * zr * zi
                cr, ci = zr, zi
                for m in range(16):
                    table[s, pl.ds(m * 8, 8), :] = cr
                    table[s, pl.ds((16 + m) * 8, 8), :] = ci
                    if m < 15:
                        cr, ci = cr * wr - ci * wi, cr * wi + ci * wr
                base.append((zr, zi))
            (ar, ai), (br, bi) = base
            pr = ar * br - ai * bi
            pi = ar * bi + ai * br
            vr = vref[s]
            vi = vref[8 + s]
            vp[s, 0] = vr * pr + vi * pi
            vp[s, 1] = vi * pr - vr * pi
        for s in range(8):
            lefts, rights = [], []
            for c in range(8):
                xs = xu[s, pl.ds(c, 32, stride=8), :]
                ys = xv[s, pl.ds(c, 32, stride=8), :]
                vr = vp[s, 0, pl.ds(c, 1), :]
                vi = vp[s, 1, pl.ds(c, 1), :]
                lefts.append(jnp.concatenate(split(jnp.concatenate([xs * vr, xs * vi], 0)), 0))
                both = jnp.concatenate([ys, ys * weight[c : c + 1]], 0)
                rights.append(jnp.concatenate(split(both), 0))
            o = lax.dot_general(
                jnp.concatenate(lefts, 1),
                jnp.concatenate(rights, 1),
                (((1,), (1,)), ((), ())),
                preferred_element_type=F32,
            )
            o = o[:64] + o[64:]
            if n == 0:
                out[s] = o if first else before[s] + o
            else:
                out[s] += o


def grant(mib):
    return pltpu.CompilerParams(vmem_limit_bytes=mib << 20)


def images(uv, chunks, before=None):
    picks = tuple(p for _, p in chunks)
    count = len(chunks)
    first = before is None
    args = [uv] + [c for c, _ in chunks] + ([] if first else [before])
    return pl.pallas_call(
        functools.partial(image_kernel, picks, first),
        out_shape=jax.ShapeDtypeStruct((8, 64, 128), F32),
        in_specs=[VM] * len(args),
        out_specs=VM,
        scratch_shapes=[
            pltpu.VMEM((8, 256, 128), F32),
            pltpu.VMEM((8, 256, 128), F32),
            pltpu.VMEM((8, 2, 8, 128), F32),
        ],
        compiler_params=grant(16),
        cost_estimate=pl.CostEstimate(
            flops=count * 200_000_000, bytes_accessed=count * 100_000, transcendentals=0
        ),
        name=f"image{count}",
    )(*args)


def pair_kernel(me_ref, inv, stations, table, taper, out):
    g = taper[pl.ds(me_ref[0], 1), :]
    for to in range(8):
        for j in range(8):
            s = inv[8 * j + to]
            p = stations[0, s]
            q = stations[1, s]
            p = p + 16 * (p >> 4)
            q = q + 16 * (q >> 4)
            pr = table[pl.ds(p, 1), :]
            pi = table[pl.ds(p + 16, 1), :]
            qr = table[pl.ds(q, 1), :]
            qi = table[pl.ds(q + 16, 1), :]
            out[to, pl.ds(j, 1), :] = (pr * qr + pi * qi) * g
            out[to, pl.ds(8 + j, 1), :] = (pi * qr - pr * qi) * g


def finish_kernel(me_ref, inv, tiles, slots, offs, acc, pair, to_image, fold, left3, right3, out, own):
    me = me_ref[0]
    owners(slots, own)
    blank = jnp.zeros((33 * 8, 128), F32)
    for b in range(4):
        out[33 * 8 * b : 33 * 8 * (b + 1), :] = blank
    first_lane = lax.broadcasted_iota(jnp.int32, (1, 128), 1) == 0
    row = lax.broadcasted_iota(jnp.int32, (8, 128), 0)
    group = lax.broadcasted_iota(jnp.int32, (8, 128), 1) // 32
    low = group == row % 4
    high = group == 3 - row % 4
    spread = [[], []]
    halves = []
    for s in range(8):
        for r in range(2):
            rows = [jnp.broadcast_to(pair[c, pl.ds(8 * r + s, 1), :], (8, 128)) for c in range(8)]
            for c in (4, 6):
                spread[r].append(jnp.where(low, jnp.where(row < 4, rows[c], rows[c + 1]), 0.0))
            for c in (3, 1):
                spread[r].append(jnp.where(high, jnp.where(row < 4, rows[c], rows[c - 1]), 0.0))
        g = acc[s]
        rc, rs, ic, js = g[0:16], g[16:32], g[32:48], g[48:64]
        real = jnp.concatenate([rc - js, rc + js], 0)
        imag = jnp.concatenate([ic + rs, ic - rs], 0)
        halves.append(jnp.concatenate([real, imag], 1))
    stack = jnp.concatenate(halves, 0)
    sh, sl = split(stack)
    img = jnp.dot(sh, to_image[...], preferred_element_type=F32) + jnp.dot(
        sl, to_image[...], preferred_element_type=F32
    )

    def unfold(r):
        h, l = split(jnp.concatenate(spread[r], 0))
        return jnp.dot(h, fold[r], preferred_element_type=F32) + jnp.dot(
            l, fold[r], preferred_element_type=F32
        )

    weighted = img * unfold(0) + pltpu.roll(img, 64, 1) * unfold(1)
    sign = jnp.where(lax.broadcasted_iota(jnp.int32, (256, 128), 1) < 64, -1.0, 1.0)
    turned = pltpu.roll(weighted, 64, 1) * sign
    wh, wl = split(weighted)
    th, tl = split(turned)

    def lanes(x):
        return jnp.concatenate([x[32 * s : 32 * s + 32] for s in range(8)], 1)

    wh, wl, th, tl = lanes(wh), lanes(wl), lanes(th), lanes(tl)
    rhs = jnp.concatenate([wh, th, wh, th, wl, tl], 0)
    half = jnp.dot(left3[...], rhs, preferred_element_type=F32)
    half = jnp.concatenate([half[:, 128 * s : 128 * s + 128] for s in range(8)], 0)
    hh, hl = split(half)
    full = jnp.dot(
        jnp.concatenate([hh, hh, hl], 1), right3[...], preferred_element_type=F32
    )
    for s in range(8):
        i = inv[8 * s + me]
        at = 33 * own[tiles[i]]
        out[pl.ds(at, 32), :] = full[32 * s : 32 * s + 32]
        out[pl.ds(at + 32, 1), :] = jnp.where(first_lane, offs[0, i], offs[1, i]).astype(F32)


def place_kernel(me_ref, arrived, keep, give, acc, spots):
    lane = lax.broadcasted_iota(jnp.int32, (32, 128), 1)
    me = me_ref[0]
    y = me >> 1
    core = me & 1
    for i in range(32):
        corner = arrived[33 * i + 32 : 33 * i + 33, :].astype(jnp.int32)
        spots[2 * i] = corner[0, 0]
        spots[2 * i + 1] = corner[0, 1]
    acc[...] = jnp.zeros_like(acc)

    def one(i, unused):
        r = spots[2 * i]
        c = spots[2 * i + 1]
        half = c >> 7
        c = c & 127
        tile = arrived[pl.ds(33 * i, 32), :]
        near = (lane >= c) & (lane < c + 32)
        moved = [pltpu.roll(tile, (c - 32 * m) & 127, 1) for m in range(4)]
        for m in range(4):
            at = (2 * m + half, pl.ds(r, 32), slice(None))
            acc[at] = acc[at] + jnp.where(near, moved[m], 0.0)

        @pl.when(c > 96)
        def _():
            far = lane < c - 96
            for m in range(4):
                at = (2 * m + 1, pl.ds(r, 32), slice(None))
                acc[at] = acc[at] + jnp.where(far, moved[m], 0.0)

        return unused

    lax.fori_loop(0, 32, one, 0)
    for d in range(4):
        block = ((y + d) & 3) << 1
        for k in range(8):
            keep[d, k] = acc[k, pl.ds(pl.multiple_of((block + core) * 32, 32), 32), :]
            give[d, k] = acc[k, pl.ds(pl.multiple_of((block + 1 - core) * 32, 32), 32), :]


def merge_kernel(keep, got, *outs):
    for d in range(4):
        outs[d][...] = keep[d] + got[d]


def last_kernel(a, b, c, d, out):
    for m in range(4):
        for half in range(2):
            k = 2 * m + half
            out[0, :, m, 128 * half : 128 * half + 128] = (a[k] + b[k]) + (c[k] + d[k])


def shift(x, dy, dc):
    pairs = [(i, ((i // 2 + dy) % 4) * 2 + (i + dc) % 2) for i in range(8)]
    return lax.ppermute(x, "ch", pairs)


def local(visibility, coordinates, freq_ratio, aterms, stations, sub_tile, offsets, tile_of_slot):
    to_image, fold, left3, right3, taper = constants()
    me = lax.axis_index("ch").astype(jnp.int32)
    me = me[None]
    stations = stations.T
    offsets = offsets.T
    own = pltpu.SMEM((32,), jnp.int32)
    shared = pl.pallas_call(
        share_kernel,
        out_shape=jax.ShapeDtypeStruct((32, 32, 128), F32),
        in_specs=[SM, VM],
        out_specs=VM,
        compiler_params=grant(4),
        name="share",
    )(me, aterms)
    sub_tile, shared = lax.optimization_barrier((sub_tile, shared))
    table = lax.all_to_all(shared.reshape(32, 4096), "bl", 0, 0, tiled=True)
    table = table.reshape(1024, 128)
    order = jnp.arange(64, dtype=jnp.int32)
    key = sub_tile * 64 + order
    pos = jnp.sum((key[None, :] < key[:, None]).astype(jnp.int32), axis=1)
    inv = jnp.sum(jnp.where(pos[None, :] == order[:, None], order[None, :], 0), axis=1)
    chunk = jax.ShapeDtypeStruct((17, 8, 128), F32)
    double = jax.ShapeDtypeStruct((2, 17, 8, 128), F32)
    mine, near, *far, uv = pl.pallas_call(
        pack_kernel,
        out_shape=[chunk, chunk, double, double, double, jax.ShapeDtypeStruct((2, 8, 128), F32)],
        in_specs=[SM, SM, SM, VM, VM],
        out_specs=[VM] * 6,
        compiler_params=grant(8),
        name="pack",
    )(me, inv, freq_ratio, visibility, coordinates)
    near = shift(near, 0, 1)
    direct = [shift(far[d - 1], d, 0) for d in range(1, 4)]
    acc = images(uv, [(mine, None), (near, None)])
    acc, *direct = lax.optimization_barrier((acc, *direct))
    swapped = [shift(x, 0, 1) for x in direct]
    acc = images(uv, [(direct[0], 0), (direct[2], 0)], acc)
    acc, table = lax.optimization_barrier((acc, table))
    pair = pl.pallas_call(
        pair_kernel,
        out_shape=jax.ShapeDtypeStruct((8, 16, 128), F32),
        in_specs=[SM, SM, SM, VM, VM],
        out_specs=VM,
        compiler_params=grant(4),
        name="pair",
    )(me, inv, stations, table, taper)
    acc, pair = lax.optimization_barrier((acc, pair))
    pair = lax.all_to_all(pair.reshape(8, 2048), "ch", 0, 0, tiled=True).reshape(8, 16, 128)
    acc = images(uv, [(swapped[0], 1), (swapped[2], 1), (direct[1], 0), (swapped[1], 1)], acc)
    outgoing = pl.pallas_call(
        finish_kernel,
        out_shape=jax.ShapeDtypeStruct((33 * 32, 128), F32),
        in_specs=[SM] * 5 + [VM] * 6,
        out_specs=VM,
        scratch_shapes=[own],
        compiler_params=grant(12),
        name="finish",
    )(me, inv, sub_tile, tile_of_slot, offsets, acc, pair, to_image, fold, left3, right3)
    arrived = lax.all_to_all(outgoing.reshape(32, 33 * 128), "bl", 0, 0, tiled=True)
    arrived = arrived.reshape(33 * 32, 128)
    half = jax.ShapeDtypeStruct((4, 8, 32, 128), F32)
    keep, give = pl.pallas_call(
        place_kernel,
        out_shape=[half, half],
        in_specs=[SM, VM],
        out_specs=[VM, VM],
        scratch_shapes=[pltpu.VMEM((8, TILE, 128), F32), pltpu.SMEM((64,), jnp.int32)],
        compiler_params=grant(8),
        name="place",
    )(me, arrived)
    got = shift(give, 0, 1)
    block = jax.ShapeDtypeStruct((8, 32, 128), F32)
    sums = pl.pallas_call(
        merge_kernel,
        out_shape=[block] * 4,
        in_specs=[VM, VM],
        out_specs=[VM] * 4,
        compiler_params=grant(6),
        name="merge",
    )(keep, got)
    parts = [sums[0]] + [shift(sums[d], d, 0) for d in range(1, 4)]
    return pl.pallas_call(
        last_kernel,
        out_shape=jax.ShapeDtypeStruct((1, 32, 4, TILE), F32),
        in_specs=[VM] * 4,
        out_specs=VM,
        compiler_params=grant(4),
        name="last",
    )(*parts)


def solution(mesh):
    placed = (
        P(None, "bl", "ch", None),
        P(None, "bl", None),
        P("ch"),
        P("bl", None),
        P("bl", None),
        P("bl"),
        P("bl", None),
        P(),
    )
    return jax.shard_map(
        local, mesh=mesh, in_specs=placed, out_specs=P("bl", "ch", None, None), check_vma=False
    )
```

```python
import functools
import math

import jax
import jax.numpy as jnp
import numpy as np
from jax import lax
from jax.experimental import pallas as pl
from jax.experimental.pallas import tpu as pltpu
from jax.sharding import PartitionSpec as P


SUB = 32
TILE = 256
F32 = jnp.float32
BF16 = jnp.bfloat16
VM = pl.BlockSpec(memory_space=pltpu.VMEM)
SM = pl.BlockSpec(memory_space=pltpu.SMEM)

INV, DEST, ST0, ST1, OFF0, OFF1, ME = 0, 64, 128, 192, 256, 320, 384

SIN = [(-1.0) ** k / math.factorial(2 * k + 1) for k in range(7)]
COS = [(-1.0) ** k / math.factorial(2 * k) for k in range(7)]


def poly(coefs, x2):
    r = jnp.full_like(x2, coefs[-1])
    for k in coefs[-2::-1]:
        r = r * x2 + k
    return r


def split(x):
    hi = x.astype(BF16)
    return hi, (x - hi.astype(F32)).astype(BF16)


def np_split(x):
    x = np.asarray(x, np.float64)
    hi = x.astype(np.float32).astype(BF16)
    lo = (x - hi.astype(np.float64)).astype(np.float32).astype(BF16)
    return hi, lo


def constants():
    pix = np.concatenate([16 + np.arange(16), 15 - np.arange(16)])
    m1 = np.zeros((2, 2, 2, 16, 2, 2, 32))
    m2 = np.zeros_like(m1)
    for b in range(32):
        n, sign = (b - 16, 1.0) if b >= 16 else (15 - b, -1.0)
        for k in range(2):
            for part in range(2):
                m1[part, k, 0, n, 0, k, b] = 1.0
                m1[part, k, 1, n, 1, k, b] = sign
                m2[part, k, 1, n, 0, k, b] = -sign
                m2[part, k, 0, n, 1, k, b] = 1.0
    to_image = np.concatenate([m1.reshape(128, 128), m2.reshape(128, 128)], 0)
    fold = np.zeros((2, 128, 128))
    for lane in range(128):
        for g in range(4):
            fold[0, lane, g * 32 + lane % 32] = 1.0
            fold[1, lane, g * 32 + lane % 32] = -1.0 if g < 2 else 1.0
    centred = np.arange(32) - 16
    four = np.exp(-2j * np.pi * centred[:, None] * centred[None, :] / 32) / 32
    left = np.concatenate([four.real[:, pix], four.imag[:, pix]], 1)
    lh, ll = np_split(left)
    left3 = np.concatenate([lh, ll, lh], 1)
    d = np.zeros((2, 2, 32, 2, 2, 32))
    for k in range(2):
        d[0, k, :, k, 0, :] = four.real.T
        d[1, k, :, k, 0, :] = -four.imag.T
        d[0, k, :, k, 1, :] = four.imag.T
        d[1, k, :, k, 1, :] = four.real.T
    dh, dl = np_split(d.reshape(128, 128))
    right3 = np.concatenate([dh, dl, dh], 0)
    line = np.sin(np.pi * (np.arange(32) + 0.5) / 32)
    taper = (line[:, None] * line[None, :]).reshape(8, 128).astype(np.float32)
    return (
        to_image.astype(BF16),
        fold.astype(BF16),
        left3.astype(BF16),
        right3.astype(BF16),
        taper,
    )


def share_kernel(me_ref, aterms, shared, strip, sems):
    me = me_ref[0]
    copies = []
    for r in range(2):
        at = pl.multiple_of(1024 * r + me * 128, 128)
        copy = pltpu.make_async_copy(aterms.at[:, pl.ds(at, 128)], strip.at[r], sems.at[r])
        copy.start()
        copies.append(copy)
    for copy in copies:
        copy.wait()
    re = strip[0]
    im = strip[1]
    for b in range(32):
        shared[b, 0:16, :] = re
        shared[b, 16:32, :] = im


def pack_kernel(ints, freq, vis, coord, *outs):
    uv = outs[5]
    me = ints[ME]
    y = me >> 1
    core = me & 1
    row = lax.broadcasted_iota(jnp.int32, (8, 128), 0)
    freqs = jnp.zeros((8, 128), F32)
    for k in range(8):
        freqs = jnp.where(row == k, freq[k], freqs)
    places = [outs[0], outs[1]] + [outs[1 + d].at[e] for d in range(1, 4) for e in range(2)]
    for q in range(8):
        to = (((y + q // 2) & 3) << 1) + ((core + q % 2) & 1)
        for j in range(8):
            s = ints[INV + 8 * j + to]
            places[q][j] = vis[0, s]
            places[q][8 + j] = vis[1, s]
        places[q][16] = freqs
    for j in range(8):
        s = ints[INV + 8 * j + me]
        for d in range(2):
            uv[d, pl.ds(j, 1), :] = coord[d, pl.ds(s, 1), :]


def image_kernel(picks, first, uv, *refs):
    count = len(picks)
    vis = [r if p is None else r.at[p] for p, r in zip(picks, refs)]
    refs = refs[count:]
    if not first:
        before = refs[0]
        refs = refs[1:]
    out, xu, xv, vp = refs
    for n in range(count):
        vref = vis[n]
        f = vref[16]
        weight = 4.0 * (f - 1.0)
        step = f * (math.pi / SUB)
        for s in range(8):
            base = []
            for d, table in ((0, xu), (1, xv)):
                phi = uv[d, pl.ds(s, 1), :] * step
                x2 = phi * phi
                zr = poly(COS, x2)
                zi = phi * poly(SIN, x2)
                turn = 4.0 * zr * zr - 2.0
                cr, ci, dr, di = zr, zi, zr, -zi
                for m in range(16):
                    table[s, pl.ds(m * 8, 8), :] = cr
                    table[s, pl.ds((16 + m) * 8, 8), :] = ci
                    cr, ci, dr, di = turn * cr - dr, turn * ci - di, cr, ci
                base.append((zr, zi))
            (ar, ai), (br, bi) = base
            pr = ar * br - ai * bi
            pi = ar * bi + ai * br
            vr = vref[s]
            vi = vref[8 + s]
            vp[s, 0] = vr * pr + vi * pi
            vp[s, 1] = vi * pr - vr * pi
        for s in range(8):
            lefts, rights = [], []
            for c in range(8):
                xs = xu[s, pl.ds(c, 32, stride=8), :]
                ys = xv[s, pl.ds(c, 32, stride=8), :]
                vr = vp[s, 0, pl.ds(c, 1), :]
                vi = vp[s, 1, pl.ds(c, 1), :]
                lefts.append(jnp.concatenate(split(jnp.concatenate([xs * vr, xs * vi], 0)), 0))
                both = jnp.concatenate([ys, ys * weight[c : c + 1]], 0)
                rights.append(jnp.concatenate(split(both), 0))
            o = lax.dot_general(
                jnp.concatenate(lefts, 1),
                jnp.concatenate(rights, 1),
                (((1,), (1,)), ((), ())),
                preferred_element_type=F32,
            )
            o = o[:64] + o[64:]
            if n == 0:
                out[s] = o if first else before[s] + o
            else:
                out[s] += o


def grant(mib):
    return pltpu.CompilerParams(vmem_limit_bytes=mib << 20)


def images(uv, chunks, before=None):
    picks = tuple(p for _, p in chunks)
    count = len(chunks)
    first = before is None
    args = [uv] + [c for c, _ in chunks] + ([] if first else [before])
    return pl.pallas_call(
        functools.partial(image_kernel, picks, first),
        out_shape=jax.ShapeDtypeStruct((8, 64, 128), F32),
        in_specs=[VM] * len(args),
        out_specs=VM,
        scratch_shapes=[
            pltpu.VMEM((8, 256, 128), F32),
            pltpu.VMEM((8, 256, 128), F32),
            pltpu.VMEM((8, 2, 8, 128), F32),
        ],
        compiler_params=grant(16),
        cost_estimate=pl.CostEstimate(
            flops=count * 200_000_000, bytes_accessed=count * 100_000, transcendentals=0
        ),
    )(*args)


def pair_kernel(ints, table, taper, out):
    g = taper[pl.ds(ints[ME], 1), :]
    for to in range(8):
        for j in range(8):
            s = ints[INV + 8 * j + to]
            p = ints[ST0 + s]
            q = ints[ST1 + s]
            p = p + 16 * (p >> 4)
            q = q + 16 * (q >> 4)
            pr = table[pl.ds(p, 1), :]
            pi = table[pl.ds(p + 16, 1), :]
            qr = table[pl.ds(q, 1), :]
            qi = table[pl.ds(q + 16, 1), :]
            out[to, pl.ds(j, 1), :] = (pr * qr + pi * qi) * g
            out[to, pl.ds(8 + j, 1), :] = (pi * qr - pr * qi) * g


def finish_kernel(ints, acc, pair, to_image, fold, left3, right3, out):
    me = ints[ME]
    blank = jnp.zeros((33 * 8, 128), F32)
    for b in range(4):
        out[33 * 8 * b : 33 * 8 * (b + 1), :] = blank
    first_lane = lax.broadcasted_iota(jnp.int32, (1, 128), 1) == 0
    row = lax.broadcasted_iota(jnp.int32, (8, 128), 0)
    group = lax.broadcasted_iota(jnp.int32, (8, 128), 1) // 32
    low = group == row % 4
    high = group == 3 - row % 4
    spread = [[], []]
    halves = []
    for s in range(8):
        for r in range(2):
            rows = [jnp.broadcast_to(pair[c, pl.ds(8 * r + s, 1), :], (8, 128)) for c in range(8)]
            for c in (4, 6):
                spread[r].append(jnp.where(low, jnp.where(row < 4, rows[c], rows[c + 1]), 0.0))
            for c in (3, 1):
                spread[r].append(jnp.where(high, jnp.where(row < 4, rows[c], rows[c - 1]), 0.0))
        g = acc[s]
        rc, rs, ic, js = g[0:16], g[16:32], g[32:48], g[48:64]
        real = jnp.concatenate([rc - js, rc + js], 0)
        imag = jnp.concatenate([ic + rs, ic - rs], 0)
        halves.append(jnp.concatenate([real, imag], 1))
    stack = jnp.concatenate(halves, 0)
    sh, sl = split(stack)
    img = jnp.dot(sh, to_image[...], preferred_element_type=F32) + jnp.dot(
        sl, to_image[...], preferred_element_type=F32
    )

    def unfold(r):
        h, l = split(jnp.concatenate(spread[r], 0))
        return jnp.dot(h, fold[r], preferred_element_type=F32) + jnp.dot(
            l, fold[r], preferred_element_type=F32
        )

    weighted = img * unfold(0) + pltpu.roll(img, 64, 1) * unfold(1)
    sign = jnp.where(lax.broadcasted_iota(jnp.int32, (256, 128), 1) < 64, -1.0, 1.0)
    turned = pltpu.roll(weighted, 64, 1) * sign
    wh, wl = split(weighted)
    th, tl = split(turned)

    def lanes(x):
        return jnp.concatenate([x[32 * s : 32 * s + 32] for s in range(8)], 1)

    wh, wl, th, tl = lanes(wh), lanes(wl), lanes(th), lanes(tl)
    rhs = jnp.concatenate([wh, th, wh, th, wl, tl], 0)
    half = jnp.dot(left3[...], rhs, preferred_element_type=F32)
    half = jnp.concatenate([half[:, 128 * s : 128 * s + 128] for s in range(8)], 0)
    hh, hl = split(half)
    full = jnp.dot(
        jnp.concatenate([hh, hh, hl], 1), right3[...], preferred_element_type=F32
    )
    for s in range(8):
        i = ints[INV + 8 * s + me]
        at = 33 * ints[DEST + i]
        out[pl.ds(at, 32), :] = full[32 * s : 32 * s + 32]
        out[pl.ds(at + 32, 1), :] = jnp.where(first_lane, ints[OFF0 + i], ints[OFF1 + i]).astype(F32)


def place_kernel(me_ref, arrived, keep, give, acc, spots):
    lane = lax.broadcasted_iota(jnp.int32, (32, 128), 1)
    me = me_ref[0]
    y = me >> 1
    core = me & 1
    for i in range(32):
        corner = arrived[33 * i + 32 : 33 * i + 33, :].astype(jnp.int32)
        spots[2 * i] = corner[0, 0]
        spots[2 * i + 1] = corner[0, 1]
    acc[...] = jnp.zeros_like(acc)

    def one(i, unused):
        r = spots[2 * i]
        c = spots[2 * i + 1]
        half = c >> 7
        c = c & 127
        tile = arrived[pl.ds(33 * i, 32), :]
        near = (lane >= c) & (lane < c + 32)
        moved = [pltpu.roll(tile, (c - 32 * m) & 127, 1) for m in range(4)]
        for m in range(4):
            at = (2 * m + half, pl.ds(r, 32), slice(None))
            acc[at] = acc[at] + jnp.where(near, moved[m], 0.0)

        @pl.when(c > 96)
        def _():
            far = lane < c - 96
            for m in range(4):
                at = (2 * m + 1, pl.ds(r, 32), slice(None))
                acc[at] = acc[at] + jnp.where(far, moved[m], 0.0)

        return unused

    lax.fori_loop(0, 32, one, 0, unroll=4)
    for d in range(4):
        block = ((y + d) & 3) << 1
        for k in range(8):
            keep[d, k] = acc[k, pl.ds(pl.multiple_of((block + core) * 32, 32), 32), :]
            give[d, k] = acc[k, pl.ds(pl.multiple_of((block + 1 - core) * 32, 32), 32), :]


def merge_kernel(keep, got, *outs):
    for d in range(4):
        outs[d][...] = keep[d] + got[d]


def last_kernel(a, b, c, d, out):
    for m in range(4):
        for half in range(2):
            k = 2 * m + half
            out[0, :, m, 128 * half : 128 * half + 128] = (a[k] + b[k]) + (c[k] + d[k])


def shift(x, dy, dc):
    pairs = [(i, ((i // 2 + dy) % 4) * 2 + (i + dc) % 2) for i in range(8)]
    return lax.ppermute(x, "ch", pairs)


def local(visibility, coordinates, freq_ratio, aterms, stations, sub_tile, offsets, tile_of_slot):
    to_image, fold, left3, right3, taper = constants()
    me = lax.axis_index("ch").astype(jnp.int32)
    me = me[None]
    shared = pl.pallas_call(
        share_kernel,
        out_shape=jax.ShapeDtypeStruct((32, 32, 128), F32),
        in_specs=[SM, pl.BlockSpec(memory_space=pltpu.HBM)],
        out_specs=VM,
        scratch_shapes=[pltpu.VMEM((2, 16, 128), F32), pltpu.SemaphoreType.DMA((2,))],
        compiler_params=grant(60),
        name="share",
    )(me, aterms)
    sub_tile, tile_of_slot, shared = lax.optimization_barrier((sub_tile, tile_of_slot, shared))
    table = lax.all_to_all(shared.reshape(32, 4096), "bl", 0, 0, tiled=True)
    table = table.reshape(1024, 128)
    order = jnp.arange(64, dtype=jnp.int32)
    hits = tile_of_slot[None, :] == sub_tile[:, None]
    dest = jnp.sum(jnp.where(hits, jnp.arange(32, dtype=jnp.int32)[None, :], 0), axis=1)
    key = dest * 64 + order
    pos = jnp.sum((key[None, :] < key[:, None]).astype(jnp.int32), axis=1)
    inv = jnp.sum(jnp.where(pos[None, :] == order[:, None], order[None, :], 0), axis=1)
    ints = jnp.concatenate(
        [
            inv,
            dest,
            stations[:, 0],
            stations[:, 1],
            offsets[:, 0],
            offsets[:, 1],
            me,
        ]
    )
    chunk = jax.ShapeDtypeStruct((17, 8, 128), F32)
    double = jax.ShapeDtypeStruct((2, 17, 8, 128), F32)
    mine, near, *far, uv = pl.pallas_call(
        pack_kernel,
        out_shape=[chunk, chunk, double, double, double, jax.ShapeDtypeStruct((2, 8, 128), F32)],
        in_specs=[SM, SM, VM, VM],
        out_specs=[VM] * 6,
        compiler_params=grant(8),
        name="pack",
    )(ints, freq_ratio, visibility, coordinates)
    near = shift(near, 0, 1)
    direct = [shift(far[d - 1], d, 0) for d in range(1, 4)]
    acc = images(uv, [(mine, None), (near, None)])
    acc, *direct = lax.optimization_barrier((acc, *direct))
    swapped = [shift(x, 0, 1) for x in direct]
    acc = images(uv, [(direct[0], 0), (direct[2], 0)], acc)
    acc, table = lax.optimization_barrier((acc, table))
    pair = pl.pallas_call(
        pair_kernel,
        out_shape=jax.ShapeDtypeStruct((8, 16, 128), F32),
        in_specs=[SM, VM, VM],
        out_specs=VM,
        compiler_params=grant(4),
        name="pair",
    )(ints, table, taper)
    acc, pair = lax.optimization_barrier((acc, pair))
    pair = lax.all_to_all(pair.reshape(8, 2048), "ch", 0, 0, tiled=True).reshape(8, 16, 128)
    acc = images(uv, [(swapped[0], 1), (swapped[2], 1), (direct[1], 0), (swapped[1], 1)], acc)
    outgoing = pl.pallas_call(
        finish_kernel,
        out_shape=jax.ShapeDtypeStruct((33 * 32, 128), F32),
        in_specs=[SM] + [VM] * 6,
        out_specs=VM,
        compiler_params=grant(12),
        name="finish",
    )(ints, acc, pair, to_image, fold, left3, right3)
    arrived = lax.all_to_all(outgoing.reshape(32, 33 * 128), "bl", 0, 0, tiled=True)
    arrived = arrived.reshape(33 * 32, 128)
    half = jax.ShapeDtypeStruct((4, 8, 32, 128), F32)
    keep, give = pl.pallas_call(
        place_kernel,
        out_shape=[half, half],
        in_specs=[SM, VM],
        out_specs=[VM, VM],
        scratch_shapes=[pltpu.VMEM((8, TILE, 128), F32), pltpu.SMEM((64,), jnp.int32)],
        compiler_params=grant(8),
        name="place",
    )(me, arrived)
    got = shift(give, 0, 1)
    block = jax.ShapeDtypeStruct((8, 32, 128), F32)
    sums = pl.pallas_call(
        merge_kernel,
        out_shape=[block] * 4,
        in_specs=[VM, VM],
        out_specs=[VM] * 4,
        compiler_params=grant(6),
        name="merge",
    )(keep, got)
    parts = [sums[0]] + [shift(sums[d], d, 0) for d in range(1, 4)]
    return pl.pallas_call(
        last_kernel,
        out_shape=jax.ShapeDtypeStruct((1, 32, 4, TILE), F32),
        in_specs=[VM] * 4,
        out_specs=VM,
        compiler_params=grant(4),
        name="last",
    )(*parts)


def solution(mesh):
    placed = (
        P(None, "bl", "ch", None),
        P(None, "bl", None),
        P("ch"),
        P("bl", None),
        P("bl", None),
        P("bl"),
        P("bl", None),
        P(),
    )
    return jax.shard_map(
        local, mesh=mesh, in_specs=placed, out_specs=P("bl", "ch", None, None), check_vma=False
    )
```

```python
import functools
import math

import jax
import jax.numpy as jnp
import numpy as np
from jax import lax
from jax.experimental import pallas as pl
from jax.experimental.pallas import tpu as pltpu
from jax.sharding import PartitionSpec as P


SUB = 32
TILE = 256
F32 = jnp.float32
BF16 = jnp.bfloat16
VM = pl.BlockSpec(memory_space=pltpu.VMEM)
SM = pl.BlockSpec(memory_space=pltpu.SMEM)

INV, DEST, ST0, ST1, OFF0, OFF1, ME = 0, 64, 128, 192, 256, 320, 384

SIN = [(-1.0) ** k / math.factorial(2 * k + 1) for k in range(7)]
COS = [(-1.0) ** k / math.factorial(2 * k) for k in range(7)]


def poly(coefs, x2):
    r = jnp.full_like(x2, coefs[-1])
    for k in coefs[-2::-1]:
        r = r * x2 + k
    return r


def split(x):
    hi = x.astype(BF16)
    return hi, (x - hi.astype(F32)).astype(BF16)


def np_split(x):
    x = np.asarray(x, np.float64)
    hi = x.astype(np.float32).astype(BF16)
    lo = (x - hi.astype(np.float64)).astype(np.float32).astype(BF16)
    return hi, lo


def constants():
    pix = np.concatenate([16 + np.arange(16), 15 - np.arange(16)])
    m1 = np.zeros((2, 2, 2, 16, 2, 2, 32))
    m2 = np.zeros_like(m1)
    for b in range(32):
        n, sign = (b - 16, 1.0) if b >= 16 else (15 - b, -1.0)
        for k in range(2):
            for part in range(2):
                m1[part, k, 0, n, 0, k, b] = 1.0
                m1[part, k, 1, n, 1, k, b] = sign
                m2[part, k, 1, n, 0, k, b] = -sign
                m2[part, k, 0, n, 1, k, b] = 1.0
    to_image = np.concatenate([m1.reshape(128, 128), m2.reshape(128, 128)], 0)
    fold = np.zeros((2, 128, 128))
    for lane in range(128):
        for g in range(4):
            fold[0, lane, g * 32 + lane % 32] = 1.0
            fold[1, lane, g * 32 + lane % 32] = -1.0 if g < 2 else 1.0
    centred = np.arange(32) - 16
    four = np.exp(-2j * np.pi * centred[:, None] * centred[None, :] / 32) / 32
    left = np.concatenate([four.real[:, pix], four.imag[:, pix]], 1)
    lh, ll = np_split(left)
    left3 = np.concatenate([lh, ll, lh], 1)
    d = np.zeros((2, 2, 32, 2, 2, 32))
    for k in range(2):
        d[0, k, :, k, 0, :] = four.real.T
        d[1, k, :, k, 0, :] = -four.imag.T
        d[0, k, :, k, 1, :] = four.imag.T
        d[1, k, :, k, 1, :] = four.real.T
    dh, dl = np_split(d.reshape(128, 128))
    right3 = np.concatenate([dh, dl, dh], 0)
    line = np.sin(np.pi * (np.arange(32) + 0.5) / 32)
    taper = (line[:, None] * line[None, :]).reshape(8, 128).astype(np.float32)
    return (
        to_image.astype(BF16),
        fold.astype(BF16),
        left3.astype(BF16),
        right3.astype(BF16),
        taper,
    )


def share_kernel(me_ref, aterms, shared, strip, sems):
    me = me_ref[0]
    copies = []
    for r in range(2):
        at = pl.multiple_of(1024 * r + me * 128, 128)
        copy = pltpu.make_async_copy(aterms.at[:, pl.ds(at, 128)], strip.at[r], sems.at[r])
        copy.start()
        copies.append(copy)
    for copy in copies:
        copy.wait()
    re = strip[0]
    im = strip[1]
    for b in range(32):
        shared[b, 0:16, :] = re
        shared[b, 16:32, :] = im


def pack_kernel(ints, freq, vis, coord, *outs):
    uv = outs[5]
    me = ints[ME]
    y = me >> 1
    core = me & 1
    row = lax.broadcasted_iota(jnp.int32, (8, 128), 0)
    freqs = jnp.zeros((8, 128), F32)
    for k in range(8):
        freqs = jnp.where(row == k, freq[k], freqs)
    places = [outs[0], outs[1]] + [outs[1 + d].at[e] for d in range(1, 4) for e in range(2)]
    for q in range(8):
        to = (((y + q // 2) & 3) << 1) + ((core + q % 2) & 1)
        for j in range(8):
            s = ints[INV + 8 * j + to]
            places[q][j] = vis[0, s]
            places[q][8 + j] = vis[1, s]
        places[q][16] = freqs
    for j in range(8):
        s = ints[INV + 8 * j + me]
        for d in range(2):
            uv[d, pl.ds(j, 1), :] = coord[d, pl.ds(s, 1), :]


def image_kernel(picks, first, uv, *refs):
    count = len(picks)
    vis = [r if p is None else r.at[p] for p, r in zip(picks, refs)]
    refs = refs[count:]
    if not first:
        before = refs[0]
        refs = refs[1:]
    out, xu, xv, vp = refs
    for n in range(count):
        vref = vis[n]
        f = vref[16]
        weight = 4.0 * (f - 1.0)
        step = f * (math.pi / SUB)
        for s in range(8):
            base = []
            for d, table in ((0, xu), (1, xv)):
                phi = uv[d, pl.ds(s, 1), :] * step
                x2 = phi * phi
                zr = poly(COS, x2)
                zi = phi * poly(SIN, x2)
                turn = 4.0 * zr * zr - 2.0
                cr, ci, dr, di = zr, zi, zr, -zi
                for m in range(16):
                    table[s, pl.ds(m * 8, 8), :] = cr
                    table[s, pl.ds((16 + m) * 8, 8), :] = ci
                    cr, ci, dr, di = turn * cr - dr, turn * ci - di, cr, ci
                base.append((zr, zi))
            (ar, ai), (br, bi) = base
            pr = ar * br - ai * bi
            pi = ar * bi + ai * br
            vr = vref[s]
            vi = vref[8 + s]
            vp[s, 0] = vr * pr + vi * pi
            vp[s, 1] = vi * pr - vr * pi
        for s in range(8):
            lefts, rights = [], []
            for c in range(8):
                xs = xu[s, pl.ds(c, 32, stride=8), :]
                ys = xv[s, pl.ds(c, 32, stride=8), :]
                vr = vp[s, 0, pl.ds(c, 1), :]
                vi = vp[s, 1, pl.ds(c, 1), :]
                lefts.append(jnp.concatenate(split(jnp.concatenate([xs * vr, xs * vi], 0)), 0))
                both = jnp.concatenate([ys, ys * weight[c : c + 1]], 0)
                rights.append(jnp.concatenate(split(both), 0))
            o = lax.dot_general(
                jnp.concatenate(lefts, 1),
                jnp.concatenate(rights, 1),
                (((1,), (1,)), ((), ())),
                preferred_element_type=F32,
            )
            o = o[:64] + o[64:]
            if n == 0:
                out[s] = o if first else before[s] + o
            else:
                out[s] += o


def grant(mib):
    return pltpu.CompilerParams(vmem_limit_bytes=mib << 20)


def images(uv, chunks, before=None):
    picks = tuple(p for _, p in chunks)
    count = len(chunks)
    first = before is None
    args = [uv] + [c for c, _ in chunks] + ([] if first else [before])
    return pl.pallas_call(
        functools.partial(image_kernel, picks, first),
        out_shape=jax.ShapeDtypeStruct((8, 64, 128), F32),
        in_specs=[VM] * len(args),
        out_specs=VM,
        scratch_shapes=[
            pltpu.VMEM((8, 256, 128), F32),
            pltpu.VMEM((8, 256, 128), F32),
            pltpu.VMEM((8, 2, 8, 128), F32),
        ],
        compiler_params=grant(16),
        cost_estimate=pl.CostEstimate(
            flops=count * 200_000_000, bytes_accessed=count * 100_000, transcendentals=0
        ),
    )(*args)


def pair_kernel(ints, table, taper, out):
    g = taper[pl.ds(ints[ME], 1), :]
    for to in range(8):
        for j in range(8):
            s = ints[INV + 8 * j + to]
            p = ints[ST0 + s]
            q = ints[ST1 + s]
            p = p + 16 * (p >> 4)
            q = q + 16 * (q >> 4)
            pr = table[pl.ds(p, 1), :]
            pi = table[pl.ds(p + 16, 1), :]
            qr = table[pl.ds(q, 1), :]
            qi = table[pl.ds(q + 16, 1), :]
            out[to, pl.ds(j, 1), :] = (pr * qr + pi * qi) * g
            out[to, pl.ds(8 + j, 1), :] = (pi * qr - pr * qi) * g


def finish_kernel(ints, acc, pair, to_image, fold, left3, right3, out):
    me = ints[ME]
    blank = jnp.zeros((33 * 8, 128), F32)
    for b in range(4):
        out[33 * 8 * b : 33 * 8 * (b + 1), :] = blank
    first_lane = lax.broadcasted_iota(jnp.int32, (1, 128), 1) == 0
    row = lax.broadcasted_iota(jnp.int32, (8, 128), 0)
    group = lax.broadcasted_iota(jnp.int32, (8, 128), 1) // 32
    low = group == row % 4
    high = group == 3 - row % 4
    spread = [[], []]
    halves = []
    for s in range(8):
        for r in range(2):
            rows = [jnp.broadcast_to(pair[c, pl.ds(8 * r + s, 1), :], (8, 128)) for c in range(8)]
            for c in (4, 6):
                spread[r].append(jnp.where(low, jnp.where(row < 4, rows[c], rows[c + 1]), 0.0))
            for c in (3, 1):
                spread[r].append(jnp.where(high, jnp.where(row < 4, rows[c], rows[c - 1]), 0.0))
        g = acc[s]
        rc, rs, ic, js = g[0:16], g[16:32], g[32:48], g[48:64]
        real = jnp.concatenate([rc - js, rc + js], 0)
        imag = jnp.concatenate([ic + rs, ic - rs], 0)
        halves.append(jnp.concatenate([real, imag], 1))
    stack = jnp.concatenate(halves, 0)
    sh, sl = split(stack)
    img = jnp.dot(sh, to_image[...], preferred_element_type=F32) + jnp.dot(
        sl, to_image[...], preferred_element_type=F32
    )

    def unfold(r):
        h, l = split(jnp.concatenate(spread[r], 0))
        return jnp.dot(h, fold[r], preferred_element_type=F32) + jnp.dot(
            l, fold[r], preferred_element_type=F32
        )

    weighted = img * unfold(0) + pltpu.roll(img, 64, 1) * unfold(1)
    sign = jnp.where(lax.broadcasted_iota(jnp.int32, (256, 128), 1) < 64, -1.0, 1.0)
    turned = pltpu.roll(weighted, 64, 1) * sign
    wh, wl = split(weighted)
    th, tl = split(turned)

    def lanes(x):
        return jnp.concatenate([x[32 * s : 32 * s + 32] for s in range(8)], 1)

    wh, wl, th, tl = lanes(wh), lanes(wl), lanes(th), lanes(tl)
    rhs = jnp.concatenate([wh, th, wh, th, wl, tl], 0)
    half = jnp.dot(left3[...], rhs, preferred_element_type=F32)
    half = jnp.concatenate([half[:, 128 * s : 128 * s + 128] for s in range(8)], 0)
    hh, hl = split(half)
    full = jnp.dot(
        jnp.concatenate([hh, hh, hl], 1), right3[...], preferred_element_type=F32
    )
    for s in range(8):
        i = ints[INV + 8 * s + me]
        at = 33 * ints[DEST + i]
        out[pl.ds(at, 32), :] = full[32 * s : 32 * s + 32]
        out[pl.ds(at + 32, 1), :] = jnp.where(first_lane, ints[OFF0 + i], ints[OFF1 + i]).astype(F32)


def place_kernel(me_ref, arrived, keep, give, acc, spots):
    lane = lax.broadcasted_iota(jnp.int32, (32, 128), 1)
    me = me_ref[0]
    y = me >> 1
    core = me & 1
    for i in range(32):
        corner = arrived[33 * i + 32 : 33 * i + 33, :].astype(jnp.int32)
        spots[2 * i] = corner[0, 0]
        spots[2 * i + 1] = corner[0, 1]
    acc[...] = jnp.zeros_like(acc)

    def one(i, unused):
        r = spots[2 * i]
        c = spots[2 * i + 1]
        half = c >> 7
        c = c & 127
        tile = arrived[pl.ds(33 * i, 32), :]
        near = (lane >= c) & (lane < c + 32)
        moved = [pltpu.roll(tile, (c - 32 * m) & 127, 1) for m in range(4)]
        for m in range(4):
            at = (2 * m + half, pl.ds(r, 32), slice(None))
            acc[at] = acc[at] + jnp.where(near, moved[m], 0.0)

        far = lane < c - 96
        for m in range(4):
            at = (2 * m + 1, pl.ds(r, 32), slice(None))
            acc[at] = acc[at] + jnp.where(far, moved[m], 0.0)
        return unused

    lax.fori_loop(0, 32, one, 0, unroll=4)
    for d in range(4):
        block = ((y + d) & 3) << 1
        for k in range(8):
            keep[d, k] = acc[k, pl.ds(pl.multiple_of((block + core) * 32, 32), 32), :]
            give[d, k] = acc[k, pl.ds(pl.multiple_of((block + 1 - core) * 32, 32), 32), :]


def merge_kernel(keep, got, *outs):
    for d in range(4):
        outs[d][...] = keep[d] + got[d]


def last_kernel(a, b, c, d, out):
    for m in range(4):
        for half in range(2):
            k = 2 * m + half
            out[0, :, m, 128 * half : 128 * half + 128] = (a[k] + b[k]) + (c[k] + d[k])


def shift(x, dy, dc):
    pairs = [(i, ((i // 2 + dy) % 4) * 2 + (i + dc) % 2) for i in range(8)]
    return lax.ppermute(x, "ch", pairs)


def local(visibility, coordinates, freq_ratio, aterms, stations, sub_tile, offsets, tile_of_slot):
    to_image, fold, left3, right3, taper = constants()
    me = lax.axis_index("ch").astype(jnp.int32)
    me = me[None]
    shared = pl.pallas_call(
        share_kernel,
        out_shape=jax.ShapeDtypeStruct((32, 32, 128), F32),
        in_specs=[SM, pl.BlockSpec(memory_space=pltpu.HBM)],
        out_specs=VM,
        scratch_shapes=[pltpu.VMEM((2, 16, 128), F32), pltpu.SemaphoreType.DMA((2,))],
        compiler_params=grant(60),
        name="share",
    )(me, aterms)
    sub_tile, tile_of_slot, shared = lax.optimization_barrier((sub_tile, tile_of_slot, shared))
    table = lax.all_to_all(shared.reshape(32, 4096), "bl", 0, 0, tiled=True)
    table = table.reshape(1024, 128)
    order = jnp.arange(64, dtype=jnp.int32)
    hits = tile_of_slot[None, :] == sub_tile[:, None]
    dest = jnp.sum(jnp.where(hits, jnp.arange(32, dtype=jnp.int32)[None, :], 0), axis=1)
    key = dest * 64 + order
    pos = jnp.sum((key[None, :] < key[:, None]).astype(jnp.int32), axis=1)
    inv = jnp.sum(jnp.where(pos[None, :] == order[:, None], order[None, :], 0), axis=1)
    ints = jnp.concatenate(
        [
            inv,
            dest,
            stations[:, 0],
            stations[:, 1],
            offsets[:, 0],
            offsets[:, 1],
            me,
        ]
    )
    chunk = jax.ShapeDtypeStruct((17, 8, 128), F32)
    double = jax.ShapeDtypeStruct((2, 17, 8, 128), F32)
    mine, near, *far, uv = pl.pallas_call(
        pack_kernel,
        out_shape=[chunk, chunk, double, double, double, jax.ShapeDtypeStruct((2, 8, 128), F32)],
        in_specs=[SM, SM, VM, VM],
        out_specs=[VM] * 6,
        compiler_params=grant(8),
        name="pack",
    )(ints, freq_ratio, visibility, coordinates)
    near = shift(near, 0, 1)
    direct = [shift(far[d - 1], d, 0) for d in range(1, 4)]
    acc = images(uv, [(mine, None), (near, None)])
    acc, one, three = lax.optimization_barrier((acc, direct[0], direct[2]))
    swap_one, swap_three = shift(one, 0, 1), shift(three, 0, 1)
    acc = images(uv, [(one, 0), (three, 0)], acc)
    acc, two = lax.optimization_barrier((acc, direct[1]))
    swap_two = shift(two, 0, 1)
    acc, table = lax.optimization_barrier((acc, table))
    pair = pl.pallas_call(
        pair_kernel,
        out_shape=jax.ShapeDtypeStruct((8, 16, 128), F32),
        in_specs=[SM, VM, VM],
        out_specs=VM,
        compiler_params=grant(4),
        name="pair",
    )(ints, table, taper)
    acc, pair = lax.optimization_barrier((acc, pair))
    pair = lax.all_to_all(pair.reshape(8, 2048), "ch", 0, 0, tiled=True).reshape(8, 16, 128)
    acc = images(uv, [(swap_one, 1), (swap_three, 1), (two, 0), (swap_two, 1)], acc)
    outgoing = pl.pallas_call(
        finish_kernel,
        out_shape=jax.ShapeDtypeStruct((33 * 32, 128), F32),
        in_specs=[SM] + [VM] * 6,
        out_specs=VM,
        compiler_params=grant(12),
        name="finish",
    )(ints, acc, pair, to_image, fold, left3, right3)
    arrived = lax.all_to_all(outgoing.reshape(32, 33 * 128), "bl", 0, 0, tiled=True)
    arrived = arrived.reshape(33 * 32, 128)
    half = jax.ShapeDtypeStruct((4, 8, 32, 128), F32)
    keep, give = pl.pallas_call(
        place_kernel,
        out_shape=[half, half],
        in_specs=[SM, VM],
        out_specs=[VM, VM],
        scratch_shapes=[pltpu.VMEM((8, TILE, 128), F32), pltpu.SMEM((64,), jnp.int32)],
        compiler_params=grant(8),
        name="place",
    )(me, arrived)
    got = shift(give, 0, 1)
    block = jax.ShapeDtypeStruct((8, 32, 128), F32)
    sums = pl.pallas_call(
        merge_kernel,
        out_shape=[block] * 4,
        in_specs=[VM, VM],
        out_specs=[VM] * 4,
        compiler_params=grant(6),
        name="merge",
    )(keep, got)
    parts = [sums[0]] + [shift(sums[d], d, 0) for d in range(1, 4)]
    return pl.pallas_call(
        last_kernel,
        out_shape=jax.ShapeDtypeStruct((1, 32, 4, TILE), F32),
        in_specs=[VM] * 4,
        out_specs=VM,
        compiler_params=grant(4),
        name="last",
    )(*parts)


def solution(mesh):
    placed = (
        P(None, "bl", "ch", None),
        P(None, "bl", None),
        P("ch"),
        P("bl", None),
        P("bl", None),
        P("bl"),
        P("bl", None),
        P(),
    )
    return jax.shard_map(
        local, mesh=mesh, in_specs=placed, out_specs=P("bl", "ch", None, None), check_vma=False
    )
```

```python
import functools
import math

import jax
import jax.numpy as jnp
import numpy as np
from jax import lax
from jax.experimental import pallas as pl
from jax.experimental.pallas import tpu as pltpu
from jax.sharding import PartitionSpec as P


SUB = 32
TILE = 256
F32 = jnp.float32
BF16 = jnp.bfloat16
VM = pl.BlockSpec(memory_space=pltpu.VMEM)
SM = pl.BlockSpec(memory_space=pltpu.SMEM)

INV, DEST, ST0, ST1, OFF0, OFF1, ME = 0, 64, 128, 192, 256, 320, 384

SIN = [(-1.0) ** k / math.factorial(2 * k + 1) for k in range(7)]
COS = [(-1.0) ** k / math.factorial(2 * k) for k in range(7)]


def poly(coefs, x2):
    r = jnp.full_like(x2, coefs[-1])
    for k in coefs[-2::-1]:
        r = r * x2 + k
    return r


def split(x):
    hi = x.astype(BF16)
    return hi, (x - hi.astype(F32)).astype(BF16)


def np_split(x):
    x = np.asarray(x, np.float64)
    hi = x.astype(np.float32).astype(BF16)
    lo = (x - hi.astype(np.float64)).astype(np.float32).astype(BF16)
    return hi, lo


def constants():
    pix = np.concatenate([16 + np.arange(16), 15 - np.arange(16)])
    m1 = np.zeros((2, 2, 2, 16, 2, 2, 32))
    m2 = np.zeros_like(m1)
    for b in range(32):
        n, sign = (b - 16, 1.0) if b >= 16 else (15 - b, -1.0)
        for k in range(2):
            for part in range(2):
                m1[part, k, 0, n, 0, k, b] = 1.0
                m1[part, k, 1, n, 1, k, b] = sign
                m2[part, k, 1, n, 0, k, b] = -sign
                m2[part, k, 0, n, 1, k, b] = 1.0
    to_image = np.concatenate([m1.reshape(128, 128), m2.reshape(128, 128)], 0)
    fold = np.zeros((2, 128, 128))
    for lane in range(128):
        for g in range(4):
            fold[0, lane, g * 32 + lane % 32] = 1.0
            fold[1, lane, g * 32 + lane % 32] = -1.0 if g < 2 else 1.0
    centred = np.arange(32) - 16
    four = np.exp(-2j * np.pi * centred[:, None] * centred[None, :] / 32) / 32
    left = np.concatenate([four.real[:, pix], four.imag[:, pix]], 1)
    lh, ll = np_split(left)
    left3 = np.concatenate([lh, ll, lh], 1)
    d = np.zeros((2, 2, 32, 2, 2, 32))
    for k in range(2):
        d[0, k, :, k, 0, :] = four.real.T
        d[1, k, :, k, 0, :] = -four.imag.T
        d[0, k, :, k, 1, :] = four.imag.T
        d[1, k, :, k, 1, :] = four.real.T
    dh, dl = np_split(d.reshape(128, 128))
    right3 = np.concatenate([dh, dl, dh], 0)
    line = np.sin(np.pi * (np.arange(32) + 0.5) / 32)
    taper = (line[:, None] * line[None, :]).reshape(8, 128).astype(np.float32)
    return (
        to_image.astype(BF16),
        fold.astype(BF16),
        left3.astype(BF16),
        right3.astype(BF16),
        taper,
    )


def share_kernel(aterms, shared, strip, sems):
    me = lax.axis_index("ch")
    copies = []
    for r in range(2):
        at = pl.multiple_of(1024 * r + me * 128, 128)
        copy = pltpu.make_async_copy(aterms.at[:, pl.ds(at, 128)], strip.at[r], sems.at[r])
        copy.start()
        copies.append(copy)
    for copy in copies:
        copy.wait()
    re = strip[0]
    im = strip[1]
    for b in range(32):
        shared[b, 0:16, :] = re
        shared[b, 16:32, :] = im


def pack_kernel(ints, freq, vis, coord, *outs):
    uv = outs[5]
    me = ints[ME]
    y = me >> 1
    core = me & 1
    row = lax.broadcasted_iota(jnp.int32, (8, 128), 0)
    freqs = jnp.zeros((8, 128), F32)
    for k in range(8):
        freqs = jnp.where(row == k, freq[k], freqs)
    places = [outs[0], outs[1]] + [outs[1 + d].at[e] for d in range(1, 4) for e in range(2)]
    for q in range(8):
        to = (((y + q // 2) & 3) << 1) + ((core + q % 2) & 1)
        for j in range(8):
            s = ints[INV + 8 * j + to]
            places[q][j] = vis[0, s]
            places[q][8 + j] = vis[1, s]
        places[q][16] = freqs
    for j in range(8):
        s = ints[INV + 8 * j + me]
        for d in range(2):
            uv[d, pl.ds(j, 1), :] = coord[d, pl.ds(s, 1), :]


def image_kernel(picks, first, uv, *refs):
    count = len(picks)
    vis = [r if p is None else r.at[p] for p, r in zip(picks, refs)]
    refs = refs[count:]
    if not first:
        before = refs[0]
        refs = refs[1:]
    out, xu, xv, vp = refs
    for n in range(count):
        vref = vis[n]
        f = vref[16]
        weight = 4.0 * (f - 1.0)
        step = f * (math.pi / SUB)
        for s in range(8):
            base = []
            for d, table in ((0, xu), (1, xv)):
                phi = uv[d, pl.ds(s, 1), :] * step
                x2 = phi * phi
                zr = poly(COS, x2)
                zi = phi * poly(SIN, x2)
                turn = 4.0 * zr * zr - 2.0
                cr, ci, dr, di = zr, zi, zr, -zi
                for m in range(16):
                    table[s, pl.ds(m * 8, 8), :] = cr
                    table[s, pl.ds((16 + m) * 8, 8), :] = ci
                    cr, ci, dr, di = turn * cr - dr, turn * ci - di, cr, ci
                base.append((zr, zi))
            (ar, ai), (br, bi) = base
            pr = ar * br - ai * bi
            pi = ar * bi + ai * br
            vr = vref[s]
            vi = vref[8 + s]
            vp[s, 0] = vr * pr + vi * pi
            vp[s, 1] = vi * pr - vr * pi
        for s in range(8):
            lefts, rights = [], []
            for c in range(8):
                xs = xu[s, pl.ds(c, 32, stride=8), :]
                ys = xv[s, pl.ds(c, 32, stride=8), :]
                vr = vp[s, 0, pl.ds(c, 1), :]
                vi = vp[s, 1, pl.ds(c, 1), :]
                lefts.append(jnp.concatenate(split(jnp.concatenate([xs * vr, xs * vi], 0)), 0))
                both = jnp.concatenate([ys, ys * weight[c : c + 1]], 0)
                rights.append(jnp.concatenate(split(both), 0))
            o = lax.dot_general(
                jnp.concatenate(lefts, 1),
                jnp.concatenate(rights, 1),
                (((1,), (1,)), ((), ())),
                preferred_element_type=F32,
            )
            o = o[:64] + o[64:]
            if n == 0:
                out[s] = o if first else before[s] + o
            else:
                out[s] += o


def grant(mib):
    return pltpu.CompilerParams(vmem_limit_bytes=mib << 20)


def images(uv, chunks, before=None):
    picks = tuple(p for _, p in chunks)
    count = len(chunks)
    first = before is None
    args = [uv] + [c for c, _ in chunks] + ([] if first else [before])
    return pl.pallas_call(
        functools.partial(image_kernel, picks, first),
        out_shape=jax.ShapeDtypeStruct((8, 64, 128), F32),
        in_specs=[VM] * len(args),
        out_specs=VM,
        scratch_shapes=[
            pltpu.VMEM((8, 256, 128), F32),
            pltpu.VMEM((8, 256, 128), F32),
            pltpu.VMEM((8, 2, 8, 128), F32),
        ],
        compiler_params=grant(16),
        cost_estimate=pl.CostEstimate(
            flops=count * 200_000_000, bytes_accessed=count * 100_000, transcendentals=0
        ),
    )(*args)


def pair_kernel(ints, table, taper, out):
    g = taper[pl.ds(ints[ME], 1), :]
    for to in range(8):
        for j in range(8):
            s = ints[INV + 8 * j + to]
            p = ints[ST0 + s]
            q = ints[ST1 + s]
            p = p + 16 * (p >> 4)
            q = q + 16 * (q >> 4)
            pr = table[pl.ds(p, 1), :]
            pi = table[pl.ds(p + 16, 1), :]
            qr = table[pl.ds(q, 1), :]
            qi = table[pl.ds(q + 16, 1), :]
            out[to, pl.ds(j, 1), :] = (pr * qr + pi * qi) * g
            out[to, pl.ds(8 + j, 1), :] = (pi * qr - pr * qi) * g


def finish_kernel(ints, acc, pair, to_image, fold, left3, right3, out):
    me = ints[ME]
    blank = jnp.zeros((33 * 8, 128), F32)
    for b in range(4):
        out[33 * 8 * b : 33 * 8 * (b + 1), :] = blank
    first_lane = lax.broadcasted_iota(jnp.int32, (1, 128), 1) == 0
    row = lax.broadcasted_iota(jnp.int32, (8, 128), 0)
    group = lax.broadcasted_iota(jnp.int32, (8, 128), 1) // 32
    low = group == row % 4
    high = group == 3 - row % 4
    spread = [[], []]
    halves = []
    for s in range(8):
        for r in range(2):
            rows = [jnp.broadcast_to(pair[c, pl.ds(8 * r + s, 1), :], (8, 128)) for c in range(8)]
            for c in (4, 6):
                spread[r].append(jnp.where(low, jnp.where(row < 4, rows[c], rows[c + 1]), 0.0))
            for c in (3, 1):
                spread[r].append(jnp.where(high, jnp.where(row < 4, rows[c], rows[c - 1]), 0.0))
        g = acc[s]
        rc, rs, ic, js = g[0:16], g[16:32], g[32:48], g[48:64]
        real = jnp.concatenate([rc - js, rc + js], 0)
        imag = jnp.concatenate([ic + rs, ic - rs], 0)
        halves.append(jnp.concatenate([real, imag], 1))
    stack = jnp.concatenate(halves, 0)
    sh, sl = split(stack)
    img = jnp.dot(sh, to_image[...], preferred_element_type=F32) + jnp.dot(
        sl, to_image[...], preferred_element_type=F32
    )

    def unfold(r):
        h, l = split(jnp.concatenate(spread[r], 0))
        return jnp.dot(h, fold[r], preferred_element_type=F32) + jnp.dot(
            l, fold[r], preferred_element_type=F32
        )

    weighted = img * unfold(0) + pltpu.roll(img, 64, 1) * unfold(1)
    sign = jnp.where(lax.broadcasted_iota(jnp.int32, (256, 128), 1) < 64, -1.0, 1.0)
    turned = pltpu.roll(weighted, 64, 1) * sign
    wh, wl = split(weighted)
    th, tl = split(turned)

    def lanes(x):
        return jnp.concatenate([x[32 * s : 32 * s + 32] for s in range(8)], 1)

    wh, wl, th, tl = lanes(wh), lanes(wl), lanes(th), lanes(tl)
    rhs = jnp.concatenate([wh, th, wh, th, wl, tl], 0)
    half = jnp.dot(left3[...], rhs, preferred_element_type=F32)
    half = jnp.concatenate([half[:, 128 * s : 128 * s + 128] for s in range(8)], 0)
    hh, hl = split(half)
    full = jnp.dot(
        jnp.concatenate([hh, hh, hl], 1), right3[...], preferred_element_type=F32
    )
    for s in range(8):
        i = ints[INV + 8 * s + me]
        at = 33 * ints[DEST + i]
        out[pl.ds(at, 32), :] = full[32 * s : 32 * s + 32]
        out[pl.ds(at + 32, 1), :] = jnp.where(first_lane, ints[OFF0 + i], ints[OFF1 + i]).astype(F32)


def place_kernel(me_ref, arrived, keep, give_two, give, acc, spots):
    gives = [give.at[0], give.at[1], give_two, give.at[2]]
    lane = lax.broadcasted_iota(jnp.int32, (32, 128), 1)
    me = me_ref[0]
    y = me >> 1
    core = me & 1
    for i in range(32):
        corner = arrived[33 * i + 32 : 33 * i + 33, :].astype(jnp.int32)
        spots[2 * i] = corner[0, 0]
        spots[2 * i + 1] = corner[0, 1]
    acc[...] = jnp.zeros_like(acc)

    def one(i, unused):
        r = spots[2 * i]
        c = spots[2 * i + 1]
        half = c >> 7
        c = c & 127
        tile = arrived[pl.ds(33 * i, 32), :]
        near = (lane >= c) & (lane < c + 32)
        moved = [pltpu.roll(tile, (c - 32 * m) & 127, 1) for m in range(4)]
        for m in range(4):
            at = (2 * m + half, pl.ds(r, 32), slice(None))
            acc[at] = acc[at] + jnp.where(near, moved[m], 0.0)

        far = lane < c - 96
        for m in range(4):
            at = (2 * m + 1, pl.ds(r, 32), slice(None))
            acc[at] = acc[at] + jnp.where(far, moved[m], 0.0)
        return unused

    lax.fori_loop(0, 32, one, 0, unroll=4)
    for d in range(4):
        block = ((y + d) & 3) << 1
        for k in range(8):
            keep[d, k] = acc[k, pl.ds(pl.multiple_of((block + core) * 32, 32), 32), :]
            gives[d][k] = acc[k, pl.ds(pl.multiple_of((block + 1 - core) * 32, 32), 32), :]


def merge_two_kernel(keep, got, out):
    out[...] = keep[2] + got[...]


def merge_kernel(keep, got, *outs):
    for i, d in enumerate((0, 1, 3)):
        outs[i][...] = keep[d] + got[i]


def last_kernel(a, b, c, d, out):
    for m in range(4):
        for half in range(2):
            k = 2 * m + half
            out[0, :, m, 128 * half : 128 * half + 128] = (a[k] + b[k]) + (c[k] + d[k])


def shift(x, dy, dc):
    pairs = [(i, ((i // 2 + dy) % 4) * 2 + (i + dc) % 2) for i in range(8)]
    return lax.ppermute(x, "ch", pairs)


def local(visibility, coordinates, freq_ratio, aterms, stations, sub_tile, offsets, tile_of_slot):
    to_image, fold, left3, right3, taper = constants()
    me = lax.axis_index("ch").astype(jnp.int32)
    me = me[None]
    shared = pl.pallas_call(
        share_kernel,
        out_shape=jax.ShapeDtypeStruct((32, 32, 128), F32),
        in_specs=[pl.BlockSpec(memory_space=pltpu.HBM)],
        out_specs=VM,
        scratch_shapes=[pltpu.VMEM((2, 16, 128), F32), pltpu.SemaphoreType.DMA((2,))],
        compiler_params=grant(60),
        name="share",
    )(aterms)
    sub_tile, tile_of_slot, shared = lax.optimization_barrier((sub_tile, tile_of_slot, shared))
    table = lax.all_to_all(shared.reshape(32, 4096), "bl", 0, 0, tiled=True)
    table = table.reshape(1024, 128)
    order = jnp.arange(64, dtype=jnp.int32)
    hits = tile_of_slot[None, :] == sub_tile[:, None]
    dest = jnp.sum(jnp.where(hits, jnp.arange(32, dtype=jnp.int32)[None, :], 0), axis=1)
    key = dest * 64 + order
    pos = jnp.sum((key[None, :] < key[:, None]).astype(jnp.int32), axis=1)
    inv = jnp.sum(jnp.where(pos[None, :] == order[:, None], order[None, :], 0), axis=1)
    ints = jnp.concatenate(
        [
            inv,
            dest,
            stations[:, 0],
            stations[:, 1],
            offsets[:, 0],
            offsets[:, 1],
            me,
        ]
    )
    chunk = jax.ShapeDtypeStruct((17, 8, 128), F32)
    double = jax.ShapeDtypeStruct((2, 17, 8, 128), F32)
    mine, near, *far, uv = pl.pallas_call(
        pack_kernel,
        out_shape=[chunk, chunk, double, double, double, jax.ShapeDtypeStruct((2, 8, 128), F32)],
        in_specs=[SM, SM, VM, VM],
        out_specs=[VM] * 6,
        compiler_params=grant(8),
        name="pack",
    )(ints, freq_ratio, visibility, coordinates)
    near = shift(near, 0, 1)
    direct = [shift(far[d - 1], d, 0) for d in range(1, 4)]
    acc = images(uv, [(mine, None), (near, None)])
    acc, one, three = lax.optimization_barrier((acc, direct[0], direct[2]))
    swap_one, swap_three = shift(one, 0, 1), shift(three, 0, 1)
    acc = images(uv, [(one, 0), (three, 0)], acc)
    acc, two = lax.optimization_barrier((acc, direct[1]))
    swap_two = shift(two, 0, 1)
    acc = images(uv, [(swap_one, 1)], acc)
    acc, table = lax.optimization_barrier((acc, table))
    pair = pl.pallas_call(
        pair_kernel,
        out_shape=jax.ShapeDtypeStruct((8, 16, 128), F32),
        in_specs=[SM, VM, VM],
        out_specs=VM,
        compiler_params=grant(4),
        name="pair",
    )(ints, table, taper)
    acc, pair = lax.optimization_barrier((acc, pair))
    pair = lax.all_to_all(pair.reshape(8, 2048), "ch", 0, 0, tiled=True).reshape(8, 16, 128)
    acc = images(uv, [(swap_three, 1), (two, 0), (swap_two, 1)], acc)
    outgoing = pl.pallas_call(
        finish_kernel,
        out_shape=jax.ShapeDtypeStruct((33 * 32, 128), F32),
        in_specs=[SM] + [VM] * 6,
        out_specs=VM,
        compiler_params=grant(12),
        name="finish",
    )(ints, acc, pair, to_image, fold, left3, right3)
    arrived = lax.all_to_all(outgoing.reshape(32, 33 * 128), "bl", 0, 0, tiled=True)
    arrived = arrived.reshape(33 * 32, 128)
    block = jax.ShapeDtypeStruct((8, 32, 128), F32)
    half = jax.ShapeDtypeStruct((4, 8, 32, 128), F32)
    rest = jax.ShapeDtypeStruct((3, 8, 32, 128), F32)
    keep, give_two, give = pl.pallas_call(
        place_kernel,
        out_shape=[half, block, rest],
        in_specs=[SM, VM],
        out_specs=[VM] * 3,
        scratch_shapes=[pltpu.VMEM((8, TILE, 128), F32), pltpu.SMEM((64,), jnp.int32)],
        compiler_params=grant(8),
        name="place",
    )(me, arrived)
    got_two = shift(give_two, 0, 1)
    got = shift(give, 0, 1)
    two = pl.pallas_call(
        merge_two_kernel,
        out_shape=block,
        in_specs=[VM, VM],
        out_specs=VM,
        compiler_params=grant(6),
        name="merge2",
    )(keep, got_two)
    two = shift(two, 2, 0)
    sums = pl.pallas_call(
        merge_kernel,
        out_shape=[block] * 3,
        in_specs=[VM, VM],
        out_specs=[VM] * 3,
        compiler_params=grant(6),
        name="merge",
    )(keep, got)
    parts = [sums[0], shift(sums[1], 1, 0), two, shift(sums[2], 3, 0)]
    return pl.pallas_call(
        last_kernel,
        out_shape=jax.ShapeDtypeStruct((1, 32, 4, TILE), F32),
        in_specs=[VM] * 4,
        out_specs=VM,
        compiler_params=grant(4),
        name="last",
    )(*parts)


def solution(mesh):
    placed = (
        P(None, "bl", "ch", None),
        P(None, "bl", None),
        P("ch"),
        P("bl", None),
        P("bl", None),
        P("bl"),
        P("bl", None),
        P(),
    )
    return jax.shard_map(
        local, mesh=mesh, in_specs=placed, out_specs=P("bl", "ch", None, None), check_vma=False
    )
```

```python
import functools
import math

import jax
import jax.numpy as jnp
import numpy as np
from jax import lax
from jax.experimental import pallas as pl
from jax.experimental.pallas import tpu as pltpu
from jax.sharding import PartitionSpec as P


SUB = 32
TILE = 256
F32 = jnp.float32
BF16 = jnp.bfloat16
VM = pl.BlockSpec(memory_space=pltpu.VMEM)
SM = pl.BlockSpec(memory_space=pltpu.SMEM)

INV, DEST, ST0, ST1, OFF0, OFF1, ME = 0, 64, 128, 192, 256, 320, 384

SIN = [(-1.0) ** k / math.factorial(2 * k + 1) for k in range(7)]
COS = [(-1.0) ** k / math.factorial(2 * k) for k in range(7)]


def poly(coefs, x2):
    r = jnp.full_like(x2, coefs[-1])
    for k in coefs[-2::-1]:
        r = r * x2 + k
    return r


def split(x):
    hi = x.astype(BF16)
    return hi, (x - hi.astype(F32)).astype(BF16)


def np_split(x):
    x = np.asarray(x, np.float64)
    hi = x.astype(np.float32).astype(BF16)
    lo = (x - hi.astype(np.float64)).astype(np.float32).astype(BF16)
    return hi, lo


def constants():
    pix = np.concatenate([16 + np.arange(16), 15 - np.arange(16)])
    m1 = np.zeros((2, 2, 2, 16, 2, 2, 32))
    m2 = np.zeros_like(m1)
    for b in range(32):
        n, sign = (b - 16, 1.0) if b >= 16 else (15 - b, -1.0)
        for k in range(2):
            for part in range(2):
                m1[part, k, 0, n, 0, k, b] = 1.0
                m1[part, k, 1, n, 1, k, b] = sign
                m2[part, k, 1, n, 0, k, b] = -sign
                m2[part, k, 0, n, 1, k, b] = 1.0
    to_image = np.concatenate([m1.reshape(128, 128), m2.reshape(128, 128)], 0)
    fold = np.zeros((2, 128, 128))
    for lane in range(128):
        for g in range(4):
            fold[0, lane, g * 32 + lane % 32] = 1.0
            fold[1, lane, g * 32 + lane % 32] = -1.0 if g < 2 else 1.0
    centred = np.arange(32) - 16
    four = np.exp(-2j * np.pi * centred[:, None] * centred[None, :] / 32) / 32
    left = np.concatenate([four.real[:, pix], four.imag[:, pix]], 1)
    lh, ll = np_split(left)
    left3 = np.concatenate([lh, ll, lh], 1)
    d = np.zeros((2, 2, 32, 2, 2, 32))
    for k in range(2):
        d[0, k, :, k, 0, :] = four.real.T
        d[1, k, :, k, 0, :] = -four.imag.T
        d[0, k, :, k, 1, :] = four.imag.T
        d[1, k, :, k, 1, :] = four.real.T
    dh, dl = np_split(d.reshape(128, 128))
    right3 = np.concatenate([dh, dl, dh], 0)
    line = np.sin(np.pi * (np.arange(32) + 0.5) / 32)
    taper = (line[:, None] * line[None, :]).reshape(8, 128).astype(np.float32)
    return (
        to_image.astype(BF16),
        fold.astype(BF16),
        left3.astype(BF16),
        right3.astype(BF16),
        taper,
    )


def share_kernel(me_ref, aterms, shared, strip, sems):
    me = me_ref[0]
    copies = []
    for r in range(2):
        at = pl.multiple_of(1024 * r + me * 128, 128)
        copy = pltpu.make_async_copy(aterms.at[:, pl.ds(at, 128)], strip.at[r], sems.at[r])
        copy.start()
        copies.append(copy)
    for copy in copies:
        copy.wait()
    re = strip[0]
    im = strip[1]
    for b in range(32):
        shared[b, 0:16, :] = re
        shared[b, 16:32, :] = im


def pack_kernel(ints, freq, vis, coord, *outs):
    uv = outs[5]
    me = ints[ME]
    y = me >> 1
    core = me & 1
    row = lax.broadcasted_iota(jnp.int32, (8, 128), 0)
    freqs = jnp.zeros((8, 128), F32)
    for k in range(8):
        freqs = jnp.where(row == k, freq[k], freqs)
    places = [outs[0], outs[1]] + [outs[1 + d].at[e] for d in range(1, 4) for e in range(2)]
    for q in range(8):
        to = (((y + q // 2) & 3) << 1) + ((core + q % 2) & 1)
        for j in range(8):
            s = ints[INV + 8 * j + to]
            places[q][j] = vis[0, s]
            places[q][8 + j] = vis[1, s]
        places[q][16] = freqs
    for j in range(8):
        s = ints[INV + 8 * j + me]
        for d in range(2):
            uv[d, pl.ds(j, 1), :] = coord[d, pl.ds(s, 1), :]


def image_kernel(picks, first, uv, *refs):
    count = len(picks)
    vis = [r if p is None else r.at[p] for p, r in zip(picks, refs)]
    refs = refs[count:]
    if not first:
        before = refs[0]
        refs = refs[1:]
    out, xu, xv, vp = refs
    for n in range(count):
        vref = vis[n]
        f = vref[16]
        weight = 4.0 * (f - 1.0)
        step = f * (math.pi / SUB)
        for s in range(8):
            base = []
            for d, table in ((0, xu), (1, xv)):
                phi = uv[d, pl.ds(s, 1), :] * step
                x2 = phi * phi
                zr = poly(COS, x2)
                zi = phi * poly(SIN, x2)
                turn = 4.0 * zr * zr - 2.0
                cr, ci, dr, di = zr, zi, zr, -zi
                for m in range(16):
                    table[s, pl.ds(m * 8, 8), :] = cr
                    table[s, pl.ds((16 + m) * 8, 8), :] = ci
                    cr, ci, dr, di = turn * cr - dr, turn * ci - di, cr, ci
                base.append((zr, zi))
            (ar, ai), (br, bi) = base
            pr = ar * br - ai * bi
            pi = ar * bi + ai * br
            vr = vref[s]
            vi = vref[8 + s]
            vp[s, 0] = vr * pr + vi * pi
            vp[s, 1] = vi * pr - vr * pi
        for s in range(8):
            lefts, rights = [], []
            for c in range(8):
                xs = xu[s, pl.ds(c, 32, stride=8), :]
                ys = xv[s, pl.ds(c, 32, stride=8), :]
                vr = vp[s, 0, pl.ds(c, 1), :]
                vi = vp[s, 1, pl.ds(c, 1), :]
                lefts.append(jnp.concatenate(split(jnp.concatenate([xs * vr, xs * vi], 0)), 0))
                both = jnp.concatenate([ys, ys * weight[c : c + 1]], 0)
                rights.append(jnp.concatenate(split(both), 0))
            o = lax.dot_general(
                jnp.concatenate(lefts, 1),
                jnp.concatenate(rights, 1),
                (((1,), (1,)), ((), ())),
                preferred_element_type=F32,
            )
            o = o[:64] + o[64:]
            if n == 0:
                out[s] = o if first else before[s] + o
            else:
                out[s] += o


def grant(mib):
    return pltpu.CompilerParams(vmem_limit_bytes=mib << 20)


def images(uv, chunks, before=None):
    picks = tuple(p for _, p in chunks)
    count = len(chunks)
    first = before is None
    args = [uv] + [c for c, _ in chunks] + ([] if first else [before])
    return pl.pallas_call(
        functools.partial(image_kernel, picks, first),
        out_shape=jax.ShapeDtypeStruct((8, 64, 128), F32),
        in_specs=[VM] * len(args),
        out_specs=VM,
        scratch_shapes=[
            pltpu.VMEM((8, 256, 128), F32),
            pltpu.VMEM((8, 256, 128), F32),
            pltpu.VMEM((8, 2, 8, 128), F32),
        ],
        compiler_params=grant(16),
        cost_estimate=pl.CostEstimate(
            flops=count * 200_000_000, bytes_accessed=count * 100_000, transcendentals=0
        ),
    )(*args)


def pair_kernel(ints, table, taper, out):
    g = taper[pl.ds(ints[ME], 1), :]
    for to in range(8):
        for j in range(8):
            s = ints[INV + 8 * j + to]
            p = ints[ST0 + s]
            q = ints[ST1 + s]
            p = p + 16 * (p >> 4)
            q = q + 16 * (q >> 4)
            pr = table[pl.ds(p, 1), :]
            pi = table[pl.ds(p + 16, 1), :]
            qr = table[pl.ds(q, 1), :]
            qi = table[pl.ds(q + 16, 1), :]
            out[to, pl.ds(j, 1), :] = (pr * qr + pi * qi) * g
            out[to, pl.ds(8 + j, 1), :] = (pi * qr - pr * qi) * g


def finish_kernel(ints, acc, pair, to_image, fold, left3, right3, out):
    me = ints[ME]
    blank = jnp.zeros((33 * 8, 128), F32)
    for b in range(4):
        out[33 * 8 * b : 33 * 8 * (b + 1), :] = blank
    first_lane = lax.broadcasted_iota(jnp.int32, (1, 128), 1) == 0
    row = lax.broadcasted_iota(jnp.int32, (8, 128), 0)
    group = lax.broadcasted_iota(jnp.int32, (8, 128), 1) // 32
    low = group == row % 4
    high = group == 3 - row % 4
    spread = [[], []]
    halves = []
    for s in range(8):
        for r in range(2):
            rows = [jnp.broadcast_to(pair[c, pl.ds(8 * r + s, 1), :], (8, 128)) for c in range(8)]
            for c in (4, 6):
                spread[r].append(jnp.where(low, jnp.where(row < 4, rows[c], rows[c + 1]), 0.0))
            for c in (3, 1):
                spread[r].append(jnp.where(high, jnp.where(row < 4, rows[c], rows[c - 1]), 0.0))
        g = acc[s]
        rc, rs, ic, js = g[0:16], g[16:32], g[32:48], g[48:64]
        real = jnp.concatenate([rc - js, rc + js], 0)
        imag = jnp.concatenate([ic + rs, ic - rs], 0)
        halves.append(jnp.concatenate([real, imag], 1))
    stack = jnp.concatenate(halves, 0)
    sh, sl = split(stack)
    img = jnp.dot(sh, to_image[...], preferred_element_type=F32) + jnp.dot(
        sl, to_image[...], preferred_element_type=F32
    )

    def unfold(r):
        h, l = split(jnp.concatenate(spread[r], 0))
        return jnp.dot(h, fold[r], preferred_element_type=F32) + jnp.dot(
            l, fold[r], preferred_element_type=F32
        )

    weighted = img * unfold(0) + pltpu.roll(img, 64, 1) * unfold(1)
    sign = jnp.where(lax.broadcasted_iota(jnp.int32, (256, 128), 1) < 64, -1.0, 1.0)
    turned = pltpu.roll(weighted, 64, 1) * sign
    wh, wl = split(weighted)
    th, tl = split(turned)

    def lanes(x):
        return jnp.concatenate([x[32 * s : 32 * s + 32] for s in range(8)], 1)

    wh, wl, th, tl = lanes(wh), lanes(wl), lanes(th), lanes(tl)
    rhs = jnp.concatenate([wh, th, wh, th, wl, tl], 0)
    half = jnp.dot(left3[...], rhs, preferred_element_type=F32)
    half = jnp.concatenate([half[:, 128 * s : 128 * s + 128] for s in range(8)], 0)
    hh, hl = split(half)
    full = jnp.dot(
        jnp.concatenate([hh, hh, hl], 1), right3[...], preferred_element_type=F32
    )
    for s in range(8):
        i = ints[INV + 8 * s + me]
        at = 33 * ints[DEST + i]
        out[pl.ds(at, 32), :] = full[32 * s : 32 * s + 32]
        out[pl.ds(at + 32, 1), :] = jnp.where(first_lane, ints[OFF0 + i], ints[OFF1 + i]).astype(F32)


def place_kernel(me_ref, arrived, keep, give, acc, spots):
    lane = lax.broadcasted_iota(jnp.int32, (32, 128), 1)
    me = me_ref[0]
    y = me >> 1
    core = me & 1
    for i in range(32):
        corner = arrived[33 * i + 32 : 33 * i + 33, :].astype(jnp.int32)
        spots[2 * i] = corner[0, 0]
        spots[2 * i + 1] = corner[0, 1]
    acc[...] = jnp.zeros_like(acc)

    def one(i, unused):
        r = spots[2 * i]
        c = spots[2 * i + 1]
        half = c >> 7
        c = c & 127
        tile = arrived[pl.ds(33 * i, 32), :]
        near = (lane >= c) & (lane < c + 32)
        moved = [pltpu.roll(tile, (c - 32 * m) & 127, 1) for m in range(4)]
        for m in range(4):
            at = (2 * m + half, pl.ds(r, 32), slice(None))
            acc[at] = acc[at] + jnp.where(near, moved[m], 0.0)

        far = lane < c - 96
        for m in range(4):
            at = (2 * m + 1, pl.ds(r, 32), slice(None))
            acc[at] = acc[at] + jnp.where(far, moved[m], 0.0)
        return unused

    lax.fori_loop(0, 32, one, 0, unroll=4)
    sign = 1 - 2 * core
    for d in range(4):
        own = (((y + sign * d) & 3) << 1) + core
        other = (((y - sign * d) & 3) << 1) + 1 - core
        for k in range(8):
            keep[d, k] = acc[k, pl.ds(pl.multiple_of(own * 32, 32), 32), :]
            give[d, k] = acc[k, pl.ds(pl.multiple_of(other * 32, 32), 32), :]


def merge_kernel(keep, got, *outs):
    for d in range(4):
        outs[d][...] = keep[d] + got[d]


def join_kernel(a, b, out):
    out[...] = a[...] + b[...]


def last_kernel(a, b, c, out):
    for m in range(4):
        for half in range(2):
            k = 2 * m + half
            out[0, :, m, 128 * half : 128 * half + 128] = a[k] + b[k] + c[k]


def shift(x, dy, dc):
    pairs = [(i, ((i // 2 + dy) % 4) * 2 + (i + dc) % 2) for i in range(8)]
    return lax.ppermute(x, "ch", pairs)


def step_y(x, way):
    pairs = [(i, ((i // 2 + way * (1 - 2 * (i % 2))) % 4) * 2 + i % 2) for i in range(8)]
    return lax.ppermute(x, "ch", pairs)


def local(visibility, coordinates, freq_ratio, aterms, stations, sub_tile, offsets, tile_of_slot):
    to_image, fold, left3, right3, taper = constants()
    me = lax.axis_index("ch").astype(jnp.int32)
    me = me[None]
    shared = pl.pallas_call(
        share_kernel,
        out_shape=jax.ShapeDtypeStruct((32, 32, 128), F32),
        in_specs=[SM, pl.BlockSpec(memory_space=pltpu.HBM)],
        out_specs=VM,
        scratch_shapes=[pltpu.VMEM((2, 16, 128), F32), pltpu.SemaphoreType.DMA((2,))],
        compiler_params=grant(60),
        name="share",
    )(me, aterms)
    sub_tile, tile_of_slot, shared = lax.optimization_barrier((sub_tile, tile_of_slot, shared))
    table = lax.all_to_all(shared.reshape(32, 4096), "bl", 0, 0, tiled=True)
    table = table.reshape(1024, 128)
    order = jnp.arange(64, dtype=jnp.int32)
    hits = tile_of_slot[None, :] == sub_tile[:, None]
    dest = jnp.sum(jnp.where(hits, jnp.arange(32, dtype=jnp.int32)[None, :], 0), axis=1)
    key = dest * 64 + order
    pos = jnp.sum((key[None, :] < key[:, None]).astype(jnp.int32), axis=1)
    inv = jnp.sum(jnp.where(pos[None, :] == order[:, None], order[None, :], 0), axis=1)
    ints = jnp.concatenate(
        [
            inv,
            dest,
            stations[:, 0],
            stations[:, 1],
            offsets[:, 0],
            offsets[:, 1],
            me,
        ]
    )
    chunk = jax.ShapeDtypeStruct((17, 8, 128), F32)
    double = jax.ShapeDtypeStruct((2, 17, 8, 128), F32)
    mine, near, *far, uv = pl.pallas_call(
        pack_kernel,
        out_shape=[chunk, chunk, double, double, double, jax.ShapeDtypeStruct((2, 8, 128), F32)],
        in_specs=[SM, SM, VM, VM],
        out_specs=[VM] * 6,
        compiler_params=grant(8),
        name="pack",
    )(ints, freq_ratio, visibility, coordinates)
    near = shift(near, 0, 1)
    direct = [shift(far[d - 1], d, 0) for d in range(1, 4)]
    acc = images(uv, [(mine, None), (near, None)])
    acc, one, three = lax.optimization_barrier((acc, direct[0], direct[2]))
    swap_one, swap_three = shift(one, 0, 1), shift(three, 0, 1)
    acc = images(uv, [(one, 0), (three, 0)], acc)
    acc, two = lax.optimization_barrier((acc, direct[1]))
    swap_two = shift(two, 0, 1)
    acc, table = lax.optimization_barrier((acc, table))
    pair = pl.pallas_call(
        pair_kernel,
        out_shape=jax.ShapeDtypeStruct((8, 16, 128), F32),
        in_specs=[SM, VM, VM],
        out_specs=VM,
        compiler_params=grant(4),
        name="pair",
    )(ints, table, taper)
    acc, pair = lax.optimization_barrier((acc, pair))
    pair = lax.all_to_all(pair.reshape(8, 2048), "ch", 0, 0, tiled=True).reshape(8, 16, 128)
    acc = images(uv, [(swap_one, 1), (swap_three, 1), (two, 0), (swap_two, 1)], acc)
    outgoing = pl.pallas_call(
        finish_kernel,
        out_shape=jax.ShapeDtypeStruct((33 * 32, 128), F32),
        in_specs=[SM] + [VM] * 6,
        out_specs=VM,
        compiler_params=grant(12),
        name="finish",
    )(ints, acc, pair, to_image, fold, left3, right3)
    arrived = lax.all_to_all(outgoing.reshape(32, 33 * 128), "bl", 0, 0, tiled=True)
    arrived = arrived.reshape(33 * 32, 128)
    half = jax.ShapeDtypeStruct((4, 8, 32, 128), F32)
    keep, give = pl.pallas_call(
        place_kernel,
        out_shape=[half, half],
        in_specs=[SM, VM],
        out_specs=[VM, VM],
        scratch_shapes=[pltpu.VMEM((8, TILE, 128), F32), pltpu.SMEM((64,), jnp.int32)],
        compiler_params=grant(8),
        name="place",
    )(me, arrived)
    got = shift(give, 0, 1)
    block = jax.ShapeDtypeStruct((8, 32, 128), F32)
    sums = pl.pallas_call(
        merge_kernel,
        out_shape=[block] * 4,
        in_specs=[VM, VM],
        out_specs=[VM] * 4,
        compiler_params=grant(6),
        name="merge",
    )(keep, got)
    relayed = step_y(sums[2], 1)
    back = step_y(sums[3], -1)
    onward = pl.pallas_call(
        join_kernel,
        out_shape=block,
        in_specs=[VM, VM],
        out_specs=VM,
        compiler_params=grant(4),
        name="join",
    )(sums[1], relayed)
    ahead = step_y(onward, 1)
    return pl.pallas_call(
        last_kernel,
        out_shape=jax.ShapeDtypeStruct((1, 32, 4, TILE), F32),
        in_specs=[VM] * 3,
        out_specs=VM,
        compiler_params=grant(4),
        name="last",
    )(sums[0], back, ahead)


def solution(mesh):
    placed = (
        P(None, "bl", "ch", None),
        P(None, "bl", None),
        P("ch"),
        P("bl", None),
        P("bl", None),
        P("bl"),
        P("bl", None),
        P(),
    )
    return jax.shard_map(
        local, mesh=mesh, in_specs=placed, out_specs=P("bl", "ch", None, None), check_vma=False
    )
```

```python
import functools
import math

import jax
import jax.numpy as jnp
import numpy as np
from jax import lax
from jax.experimental import pallas as pl
from jax.experimental.pallas import tpu as pltpu
from jax.sharding import PartitionSpec as P


SUB = 32
TILE = 256
F32 = jnp.float32
BF16 = jnp.bfloat16
VM = pl.BlockSpec(memory_space=pltpu.VMEM)
SM = pl.BlockSpec(memory_space=pltpu.SMEM)

INV, DEST, ST0, ST1, OFF0, OFF1, ME = 0, 64, 128, 192, 256, 320, 384

SIN = [(-1.0) ** k / math.factorial(2 * k + 1) for k in range(7)]
COS = [(-1.0) ** k / math.factorial(2 * k) for k in range(7)]


def poly(coefs, x2):
    r = jnp.full_like(x2, coefs[-1])
    for k in coefs[-2::-1]:
        r = r * x2 + k
    return r


def split(x):
    hi = x.astype(BF16)
    return hi, (x - hi.astype(F32)).astype(BF16)


def np_split(x):
    x = np.asarray(x, np.float64)
    hi = x.astype(np.float32).astype(BF16)
    lo = (x - hi.astype(np.float64)).astype(np.float32).astype(BF16)
    return hi, lo


def constants():
    pix = np.concatenate([16 + np.arange(16), 15 - np.arange(16)])
    m1 = np.zeros((2, 2, 2, 16, 2, 2, 32))
    m2 = np.zeros_like(m1)
    for b in range(32):
        n, sign = (b - 16, 1.0) if b >= 16 else (15 - b, -1.0)
        for k in range(2):
            for part in range(2):
                m1[part, k, 0, n, 0, k, b] = 1.0
                m1[part, k, 1, n, 1, k, b] = sign
                m2[part, k, 1, n, 0, k, b] = -sign
                m2[part, k, 0, n, 1, k, b] = 1.0
    to_image = np.concatenate([m1.reshape(128, 128), m2.reshape(128, 128)], 0)
    fold = np.zeros((2, 128, 128))
    for lane in range(128):
        for g in range(4):
            fold[0, lane, g * 32 + lane % 32] = 1.0
            fold[1, lane, g * 32 + lane % 32] = -1.0 if g < 2 else 1.0
    centred = np.arange(32) - 16
    four = np.exp(-2j * np.pi * centred[:, None] * centred[None, :] / 32) / 32
    left = np.concatenate([four.real[:, pix], four.imag[:, pix]], 1)
    lh, ll = np_split(left)
    left3 = np.concatenate([lh, ll, lh], 1)
    d = np.zeros((2, 2, 32, 2, 2, 32))
    for k in range(2):
        d[0, k, :, k, 0, :] = four.real.T
        d[1, k, :, k, 0, :] = -four.imag.T
        d[0, k, :, k, 1, :] = four.imag.T
        d[1, k, :, k, 1, :] = four.real.T
    dh, dl = np_split(d.reshape(128, 128))
    right3 = np.concatenate([dh, dl, dh], 0)
    line = np.sin(np.pi * (np.arange(32) + 0.5) / 32)
    taper = (line[:, None] * line[None, :]).reshape(8, 128).astype(np.float32)
    return (
        to_image.astype(BF16),
        fold.astype(BF16),
        left3.astype(BF16),
        right3.astype(BF16),
        taper,
    )


def share_kernel(aterms, shared, strip, sems):
    me = lax.axis_index("ch")
    copies = []
    for r in range(2):
        at = pl.multiple_of(1024 * r + me * 128, 128)
        copy = pltpu.make_async_copy(aterms.at[:, pl.ds(at, 128)], strip.at[r], sems.at[r])
        copy.start()
        copies.append(copy)
    for copy in copies:
        copy.wait()
    re = strip[0]
    im = strip[1]
    for b in range(32):
        shared[b, 0:16, :] = re
        shared[b, 16:32, :] = im


def pack_kernel(ints, freq, vis, coord, *outs):
    uv = outs[5]
    me = ints[ME]
    y = me >> 1
    core = me & 1
    row = lax.broadcasted_iota(jnp.int32, (8, 128), 0)
    freqs = jnp.zeros((8, 128), F32)
    for k in range(8):
        freqs = jnp.where(row == k, freq[k], freqs)
    places = [outs[0], outs[1]] + [outs[1 + d].at[e] for d in range(1, 4) for e in range(2)]
    for q in range(8):
        to = (((y + q // 2) & 3) << 1) + ((core + q % 2) & 1)
        for j in range(8):
            s = ints[INV + 8 * j + to]
            places[q][j] = vis[0, s]
            places[q][8 + j] = vis[1, s]
        places[q][16] = freqs
    for j in range(8):
        s = ints[INV + 8 * j + me]
        for d in range(2):
            uv[d, pl.ds(j, 1), :] = coord[d, pl.ds(s, 1), :]


def image_kernel(picks, first, uv, *refs):
    count = len(picks)
    vis = [r if p is None else r.at[p] for p, r in zip(picks, refs)]
    refs = refs[count:]
    if not first:
        before = refs[0]
        refs = refs[1:]
    out, xu, xv, vp = refs
    for n in range(count):
        vref = vis[n]
        f = vref[16]
        weight = 4.0 * (f - 1.0)
        step = f * (math.pi / SUB)
        for s in range(8):
            base = []
            for d, table in ((0, xu), (1, xv)):
                phi = uv[d, pl.ds(s, 1), :] * step
                x2 = phi * phi
                zr = poly(COS, x2)
                zi = phi * poly(SIN, x2)
                turn = 4.0 * zr * zr - 2.0
                cr, ci, dr, di = zr, zi, zr, -zi
                for m in range(16):
                    table[s, pl.ds(m * 8, 8), :] = cr
                    table[s, pl.ds((16 + m) * 8, 8), :] = ci
                    cr, ci, dr, di = turn * cr - dr, turn * ci - di, cr, ci
                base.append((zr, zi))
            (ar, ai), (br, bi) = base
            pr = ar * br - ai * bi
            pi = ar * bi + ai * br
            vr = vref[s]
            vi = vref[8 + s]
            vp[s, 0] = vr * pr + vi * pi
            vp[s, 1] = vi * pr - vr * pi
        for s in range(8):
            lefts, rights = [], []
            for c in range(8):
                xs = xu[s, pl.ds(c, 32, stride=8), :]
                ys = xv[s, pl.ds(c, 32, stride=8), :]
                vr = vp[s, 0, pl.ds(c, 1), :]
                vi = vp[s, 1, pl.ds(c, 1), :]
                lefts.append(jnp.concatenate(split(jnp.concatenate([xs * vr, xs * vi], 0)), 0))
                both = jnp.concatenate([ys, ys * weight[c : c + 1]], 0)
                rights.append(jnp.concatenate(split(both), 0))
            o = lax.dot_general(
                jnp.concatenate(lefts, 1),
                jnp.concatenate(rights, 1),
                (((1,), (1,)), ((), ())),
                preferred_element_type=F32,
            )
            o = o[:64] + o[64:]
            if n == 0:
                out[s] = o if first else before[s] + o
            else:
                out[s] += o


def grant(mib):
    return pltpu.CompilerParams(vmem_limit_bytes=mib << 20)


def images(uv, chunks, before=None):
    picks = tuple(p for _, p in chunks)
    count = len(chunks)
    first = before is None
    args = [uv] + [c for c, _ in chunks] + ([] if first else [before])
    return pl.pallas_call(
        functools.partial(image_kernel, picks, first),
        out_shape=jax.ShapeDtypeStruct((8, 64, 128), F32),
        in_specs=[VM] * len(args),
        out_specs=VM,
        scratch_shapes=[
            pltpu.VMEM((8, 256, 128), F32),
            pltpu.VMEM((8, 256, 128), F32),
            pltpu.VMEM((8, 2, 8, 128), F32),
        ],
        compiler_params=grant(16),
        cost_estimate=pl.CostEstimate(
            flops=count * 200_000_000, bytes_accessed=count * 100_000, transcendentals=0
        ),
    )(*args)


def pair_kernel(ints, table, taper, out):
    g = taper[pl.ds(ints[ME], 1), :]
    for to in range(8):
        for j in range(8):
            s = ints[INV + 8 * j + to]
            p = ints[ST0 + s]
            q = ints[ST1 + s]
            p = p + 16 * (p >> 4)
            q = q + 16 * (q >> 4)
            pr = table[pl.ds(p, 1), :]
            pi = table[pl.ds(p + 16, 1), :]
            qr = table[pl.ds(q, 1), :]
            qi = table[pl.ds(q + 16, 1), :]
            out[to, pl.ds(j, 1), :] = (pr * qr + pi * qi) * g
            out[to, pl.ds(8 + j, 1), :] = (pi * qr - pr * qi) * g


def finish_kernel(ints, acc, pair, to_image, fold, left3, right3, out):
    me = ints[ME]
    blank = jnp.zeros((33 * 8, 128), F32)
    for b in range(4):
        out[33 * 8 * b : 33 * 8 * (b + 1), :] = blank
    first_lane = lax.broadcasted_iota(jnp.int32, (1, 128), 1) == 0
    row = lax.broadcasted_iota(jnp.int32, (8, 128), 0)
    group = lax.broadcasted_iota(jnp.int32, (8, 128), 1) // 32
    low = group == row % 4
    high = group == 3 - row % 4
    spread = [[], []]
    halves = []
    for s in range(8):
        for r in range(2):
            rows = [jnp.broadcast_to(pair[c, pl.ds(8 * r + s, 1), :], (8, 128)) for c in range(8)]
            for c in (4, 6):
                spread[r].append(jnp.where(low, jnp.where(row < 4, rows[c], rows[c + 1]), 0.0))
            for c in (3, 1):
                spread[r].append(jnp.where(high, jnp.where(row < 4, rows[c], rows[c - 1]), 0.0))
        g = acc[s]
        rc, rs, ic, js = g[0:16], g[16:32], g[32:48], g[48:64]
        real = jnp.concatenate([rc - js, rc + js], 0)
        imag = jnp.concatenate([ic + rs, ic - rs], 0)
        halves.append(jnp.concatenate([real, imag], 1))
    stack = jnp.concatenate(halves, 0)
    sh, sl = split(stack)
    img = jnp.dot(sh, to_image[...], preferred_element_type=F32) + jnp.dot(
        sl, to_image[...], preferred_element_type=F32
    )

    def unfold(r):
        h, l = split(jnp.concatenate(spread[r], 0))
        return jnp.dot(h, fold[r], preferred_element_type=F32) + jnp.dot(
            l, fold[r], preferred_element_type=F32
        )

    weighted = img * unfold(0) + pltpu.roll(img, 64, 1) * unfold(1)
    sign = jnp.where(lax.broadcasted_iota(jnp.int32, (256, 128), 1) < 64, -1.0, 1.0)
    turned = pltpu.roll(weighted, 64, 1) * sign
    wh, wl = split(weighted)
    th, tl = split(turned)

    def lanes(x):
        return jnp.concatenate([x[32 * s : 32 * s + 32] for s in range(8)], 1)

    wh, wl, th, tl = lanes(wh), lanes(wl), lanes(th), lanes(tl)
    rhs = jnp.concatenate([wh, th, wh, th, wl, tl], 0)
    half = jnp.dot(left3[...], rhs, preferred_element_type=F32)
    half = jnp.concatenate([half[:, 128 * s : 128 * s + 128] for s in range(8)], 0)
    hh, hl = split(half)
    full = jnp.dot(
        jnp.concatenate([hh, hh, hl], 1), right3[...], preferred_element_type=F32
    )
    for s in range(8):
        i = ints[INV + 8 * s + me]
        at = 33 * ints[DEST + i]
        out[pl.ds(at, 32), :] = full[32 * s : 32 * s + 32]
        out[pl.ds(at + 32, 1), :] = jnp.where(first_lane, ints[OFF0 + i], ints[OFF1 + i]).astype(F32)


def place_kernel(me_ref, arrived, keep, give, acc, spots):
    lane = lax.broadcasted_iota(jnp.int32, (32, 128), 1)
    me = me_ref[0]
    y = me >> 1
    core = me & 1
    for i in range(32):
        corner = arrived[33 * i + 32 : 33 * i + 33, :].astype(jnp.int32)
        spots[2 * i] = corner[0, 0]
        spots[2 * i + 1] = corner[0, 1]
    acc[...] = jnp.zeros_like(acc)

    def one(i, unused):
        r = spots[2 * i]
        c = spots[2 * i + 1]
        half = c >> 7
        c = c & 127
        tile = arrived[pl.ds(33 * i, 32), :]
        near = (lane >= c) & (lane < c + 32)
        moved = [pltpu.roll(tile, (c - 32 * m) & 127, 1) for m in range(4)]
        for m in range(4):
            at = (2 * m + half, pl.ds(r, 32), slice(None))
            acc[at] = acc[at] + jnp.where(near, moved[m], 0.0)

        far = lane < c - 96
        for m in range(4):
            at = (2 * m + 1, pl.ds(r, 32), slice(None))
            acc[at] = acc[at] + jnp.where(far, moved[m], 0.0)
        return unused

    lax.fori_loop(0, 32, one, 0, unroll=16)
    for d in range(4):
        block = ((y + d) & 3) << 1
        for k in range(8):
            keep[d, k] = acc[k, pl.ds(pl.multiple_of((block + core) * 32, 32), 32), :]
            give[d, k] = acc[k, pl.ds(pl.multiple_of((block + 1 - core) * 32, 32), 32), :]


def merge_kernel(keep, got, *outs):
    for d in range(4):
        outs[d][...] = keep[d] + got[d]


def last_kernel(a, b, c, d, out):
    for m in range(4):
        for half in range(2):
            k = 2 * m + half
            out[0, :, m, 128 * half : 128 * half + 128] = (a[k] + b[k]) + (c[k] + d[k])


def shift(x, dy, dc):
    pairs = [(i, ((i // 2 + dy) % 4) * 2 + (i + dc) % 2) for i in range(8)]
    return lax.ppermute(x, "ch", pairs)


def local(visibility, coordinates, freq_ratio, aterms, stations, sub_tile, offsets, tile_of_slot):
    to_image, fold, left3, right3, taper = constants()
    me = lax.axis_index("ch").astype(jnp.int32)
    me = me[None]
    shared = pl.pallas_call(
        share_kernel,
        out_shape=jax.ShapeDtypeStruct((32, 32, 128), F32),
        in_specs=[pl.BlockSpec(memory_space=pltpu.HBM)],
        out_specs=VM,
        scratch_shapes=[pltpu.VMEM((2, 16, 128), F32), pltpu.SemaphoreType.DMA((2,))],
        compiler_params=grant(60),
        name="share",
    )(aterms)
    sub_tile, tile_of_slot, shared = lax.optimization_barrier((sub_tile, tile_of_slot, shared))
    table = lax.all_to_all(shared.reshape(32, 4096), "bl", 0, 0, tiled=True)
    table = table.reshape(1024, 128)
    order = jnp.arange(64, dtype=jnp.int32)
    hits = tile_of_slot[None, :] == sub_tile[:, None]
    dest = jnp.sum(jnp.where(hits, jnp.arange(32, dtype=jnp.int32)[None, :], 0), axis=1)
    key = dest * 64 + order
    pos = jnp.sum((key[None, :] < key[:, None]).astype(jnp.int32), axis=1)
    inv = jnp.sum(jnp.where(pos[None, :] == order[:, None], order[None, :], 0), axis=1)
    ints = jnp.concatenate(
        [
            inv,
            dest,
            stations[:, 0],
            stations[:, 1],
            offsets[:, 0],
            offsets[:, 1],
            me,
        ]
    )
    chunk = jax.ShapeDtypeStruct((17, 8, 128), F32)
    double = jax.ShapeDtypeStruct((2, 17, 8, 128), F32)
    mine, near, *far, uv = pl.pallas_call(
        pack_kernel,
        out_shape=[chunk, chunk, double, double, double, jax.ShapeDtypeStruct((2, 8, 128), F32)],
        in_specs=[SM, SM, VM, VM],
        out_specs=[VM] * 6,
        compiler_params=grant(8),
        name="pack",
    )(ints, freq_ratio, visibility, coordinates)
    near = shift(near, 0, 1)
    direct = [shift(far[d - 1], d, 0) for d in range(1, 4)]
    acc = images(uv, [(mine, None), (near, None)])
    acc, one, three = lax.optimization_barrier((acc, direct[0], direct[2]))
    swap_one, swap_three = shift(one, 0, 1), shift(three, 0, 1)
    acc = images(uv, [(one, 0), (three, 0)], acc)
    acc, two = lax.optimization_barrier((acc, direct[1]))
    swap_two = shift(two, 0, 1)
    acc, table = lax.optimization_barrier((acc, table))
    pair = pl.pallas_call(
        pair_kernel,
        out_shape=jax.ShapeDtypeStruct((8, 16, 128), F32),
        in_specs=[SM, VM, VM],
        out_specs=VM,
        compiler_params=grant(4),
        name="pair",
    )(ints, table, taper)
    acc, pair = lax.optimization_barrier((acc, pair))
    pair = lax.all_to_all(pair.reshape(8, 2048), "ch", 0, 0, tiled=True).reshape(8, 16, 128)
    acc = images(uv, [(swap_one, 1), (swap_three, 1), (two, 0), (swap_two, 1)], acc)
    outgoing = pl.pallas_call(
        finish_kernel,
        out_shape=jax.ShapeDtypeStruct((33 * 32, 128), F32),
        in_specs=[SM] + [VM] * 6,
        out_specs=VM,
        compiler_params=grant(12),
        name="finish",
    )(ints, acc, pair, to_image, fold, left3, right3)
    arrived = lax.all_to_all(outgoing.reshape(32, 33 * 128), "bl", 0, 0, tiled=True)
    arrived = arrived.reshape(33 * 32, 128)
    half = jax.ShapeDtypeStruct((4, 8, 32, 128), F32)
    keep, give = pl.pallas_call(
        place_kernel,
        out_shape=[half, half],
        in_specs=[SM, VM],
        out_specs=[VM, VM],
        scratch_shapes=[pltpu.VMEM((8, TILE, 128), F32), pltpu.SMEM((64,), jnp.int32)],
        compiler_params=grant(8),
        name="place",
    )(me, arrived)
    got = shift(give, 0, 1)
    block = jax.ShapeDtypeStruct((8, 32, 128), F32)
    sums = pl.pallas_call(
        merge_kernel,
        out_shape=[block] * 4,
        in_specs=[VM, VM],
        out_specs=[VM] * 4,
        compiler_params=grant(6),
        name="merge",
    )(keep, got)
    parts = [sums[0]] + [shift(sums[d], d, 0) for d in range(1, 4)]
    return pl.pallas_call(
        last_kernel,
        out_shape=jax.ShapeDtypeStruct((1, 32, 4, TILE), F32),
        in_specs=[VM] * 4,
        out_specs=VM,
        compiler_params=grant(4),
        name="last",
    )(*parts)


def solution(mesh):
    placed = (
        P(None, "bl", "ch", None),
        P(None, "bl", None),
        P("ch"),
        P("bl", None),
        P("bl", None),
        P("bl"),
        P("bl", None),
        P(),
    )
    return jax.shard_map(
        local, mesh=mesh, in_specs=placed, out_specs=P("bl", "ch", None, None), check_vma=False
    )
```
